256 devices in a mesh: dp: 64 (over z, x, core), tensor: 4 (over y).
Axes of the slice: x: 4, y: 4, z: 8, core: 2. Of those that a mesh axis runs over, the one named last changes fastest.
Arguments:
- hidden: bfloat16 [8192, 4096], P('dp', 'tensor'), may hold values from -6 to 6
- grad_out: bfloat16 [8192, 4096], P('dp', 'tensor'), may hold values from -0.59765625 to 0.59765625
- query_weight: bfloat16 [4096, 4096], P(None, 'tensor'), may hold values from -0.09375 to 0.09375
- key_weight: bfloat16 [768, 4096], P(None, 'tensor'), may hold values from -0.21875 to 0.21875
- value_weight: bfloat16 [768, 4096], P(None, 'tensor'), may hold values from -0.21875 to 0.21875
- out_weight: bfloat16 [4096, 4096], P('tensor', 'dp'), may hold values from -0.75 to 0.75
- neighbour_states: bfloat16 [256, 128, 768], P('dp', None, 'tensor'), may hold values from -6 to 6
- block_owner: int32 [64, 4], P('dp'), may hold values from 0 to 63, as said below
- slot_target: int32 [64, 4], P('dp'), may hold values from 0 to 63, as said below
Outputs:
- cross_out: bfloat16 [8192, 4096], P('dp', 'tensor')
- grad_hidden: bfloat16 [8192, 4096], P('dp', 'tensor')
- grad_states: bfloat16 [256, 128, 768], P('dp', None, 'tensor')
The draws below stay inside these ranges and needn't reach their ends.
Inputs may be any that keep to these rules, and one draw needn't show every extreme that they name: block_owner[d, t] = o exactly when slot_target[o, t] = d. The blocks 2k and 2k+1 of a dp index share their holder; the difference (holder - d) modulo the dp count is the same for every d, lies in 1 to 4, and differs between k. So a dp index holds exactly 2 blocks for each of 2 other indices. `slot_target`: the inverse map of block_owner, as stated there.
All inputs are finite; a program needn't handle non-finite values.
Results may differ from the reference program's by a relative error of at most 0.012.
Values may be sent and summed in bfloat16 or wider, within the bound.
No kernel may reach another device: no remote copies, remote signals or barrier semaphores. Data moves between devices by JAX's collectives and lax.ppermute only.
A program may use at most 128 MiB of HBM per device.

```python
import math
import jax
import jax.numpy as jnp
from jax import lax

D = 4096
HEADS = 32
HD = 128
DE = 768
SPAN = 64
NBR = 128
K_NB = 2
CH_DEV = 2
WINDOW = 4
NEED = 4
TOKENS = 8192
BLOCKS = 256
N_DP = 64
N_TENSOR = 4


def owner_offsets(key):
    shuffled = jax.random.permutation(jax.random.fold_in(key, 11), WINDOW)
    return jnp.repeat(shuffled[:CH_DEV] + 1, K_NB).astype(jnp.int32)


def draw_block_owner(key, part):
    offsets = owner_offsets(key)
    device_ids = jnp.arange(N_DP, dtype=jnp.int32)[:, None]
    return ((device_ids + offsets[None, :]) % N_DP).astype(jnp.int32)


def draw_slot_target(key, part):
    offsets = owner_offsets(key)
    device_ids = jnp.arange(N_DP, dtype=jnp.int32)[:, None]
    return ((device_ids - offsets[None, :] + N_DP) % N_DP).astype(jnp.int32)


def shard_levels(stream_key, dims, pieces, smallest, largest):
    factor_of, own = 1.0, jax.random.fold_in(stream_key, 6)
    for position, parts in pieces:
        heights = jnp.exp(jax.random.uniform(jax.random.fold_in(own, position), (parts,), jnp.float32, smallest / len(pieces), largest / len(pieces)))
        factor_of = factor_of * jnp.repeat(heights, dims[position] // parts).reshape([-1 if axis == position else 1 for axis in range(len(dims))])
    return factor_of


def bell_draw(stream_key, dims, spread, bound, shards=(), kind=jnp.bfloat16):
    array = spread * jax.random.normal(stream_key, dims, jnp.float32)
    if shards:
        array = array * shard_levels(stream_key, dims, shards, -0.22, 0.18)
    return jnp.clip(array, -bound, bound).astype(kind)


def setup_inputs(seed: int = 0) -> dict:
    key_list = jax.random.split(jax.random.key(seed), 10)
    hidden = bell_draw(key_list[0], (TOKENS, D), 1.0, 6.0, ((0, 64), (1, 4)))
    grad_out = bell_draw(key_list[1], (TOKENS, D), 0.1, 0.59765625, ((0, 64), (1, 4)))
    query_weight = bell_draw(key_list[2], (D, D), D ** -0.5, 0.09375, ((1, 4),))
    key_weight = bell_draw(key_list[3], (DE, D), DE ** -0.5, 0.21875, ((1, 4),))
    value_weight = bell_draw(key_list[4], (DE, D), DE ** -0.5, 0.21875, ((1, 4),))
    out_weight = bell_draw(key_list[5], (D, D), 64 ** -0.5, 0.75, ((0, 4), (1, 64)))
    neighbour_states = bell_draw(key_list[6], (BLOCKS, NBR, DE), 1.0, 6.0, ((0, 64), (2, 4)))
    block_owner = draw_block_owner(jax.random.fold_in(key_list[9], 71), 0)
    slot_target = draw_slot_target(jax.random.fold_in(key_list[9], 71), 0)
    return {"hidden": hidden, "grad_out": grad_out, "query_weight": query_weight, "key_weight": key_weight, "value_weight": value_weight, "out_weight": out_weight, "neighbour_states": neighbour_states, "block_owner": block_owner, "slot_target": slot_target}


def grouped_sum(left, right_t, groups):
    width = left.shape[1] // groups
    total = jnp.zeros((left.shape[0], right_t.shape[1]), jnp.float32)
    for group in range(groups):
        piece = jnp.dot(left[:, group * width:(group + 1) * width], right_t[group * width:(group + 1) * width, :], preferred_element_type=jnp.float32)
        total = total + piece.astype(jnp.bfloat16).astype(jnp.float32)
    return total

def reference(hidden, grad_out, query_weight, key_weight, value_weight, out_weight, neighbour_states, block_owner, slot_target):
    block_ids = jnp.arange(NEED, dtype=jnp.int32)
    rows_in = (block_owner * NEED + block_ids[None, :]).reshape(-1).astype(jnp.int32)
    neighbours = jnp.take(neighbour_states, rows_in, axis=0)
    span_count = TOKENS // SPAN
    score_scale = 1.0 / math.sqrt(HD)
    query = jnp.dot(hidden, query_weight, preferred_element_type=jnp.float32).astype(jnp.bfloat16)
    flat_states = neighbours.reshape(-1, DE)
    key = jnp.dot(flat_states, key_weight, preferred_element_type=jnp.float32).astype(jnp.bfloat16)
    value = jnp.dot(flat_states, value_weight, preferred_element_type=jnp.float32).astype(jnp.bfloat16)
    query_heads = query.astype(jnp.float32).reshape(span_count, SPAN, HEADS, HD)
    key_heads = key.astype(jnp.float32).reshape(span_count, K_NB * NBR, HEADS, HD)
    value_heads = value.astype(jnp.float32).reshape(span_count, K_NB * NBR, HEADS, HD)
    scores = jnp.einsum('cqhd,ckhd->chqk', query_heads, key_heads) * score_scale
    highest = lax.optimization_barrier(jnp.max(scores, axis=-1, keepdims=True))
    expanded = jnp.exp(scores - highest)
    probs = expanded / lax.optimization_barrier(jnp.sum(expanded, axis=-1, keepdims=True))
    probs_low = probs.astype(jnp.bfloat16)
    attended = jnp.einsum('chqk,ckhd->cqhd', probs_low.astype(jnp.float32), value_heads).astype(jnp.bfloat16).reshape(TOKENS, D)
    cross_out = grouped_sum(attended, out_weight, N_TENSOR).astype(jnp.bfloat16)
    grad_attended = jnp.dot(grad_out, out_weight.T, preferred_element_type=jnp.float32).astype(jnp.bfloat16)
    grad_heads = grad_attended.astype(jnp.float32).reshape(span_count, SPAN, HEADS, HD)
    grad_probs = jnp.einsum('cqhd,ckhd->chqk', grad_heads, value_heads)
    grad_scores = (probs * (grad_probs - lax.optimization_barrier(jnp.sum(probs * grad_probs, axis=-1, keepdims=True))) * score_scale).astype(jnp.bfloat16)
    grad_scores_f = grad_scores.astype(jnp.float32)
    grad_query = jnp.einsum('chqk,ckhd->cqhd', grad_scores_f, key_heads).astype(jnp.bfloat16).reshape(TOKENS, D)
    grad_key = jnp.einsum('chqk,cqhd->ckhd', grad_scores_f, query_heads).astype(jnp.bfloat16).reshape(-1, D)
    grad_value = jnp.einsum('chqk,cqhd->ckhd', probs_low.astype(jnp.float32), grad_heads).astype(jnp.bfloat16).reshape(-1, D)
    grad_hidden = grouped_sum(grad_query, query_weight.T, N_TENSOR).astype(jnp.bfloat16)
    width = D // N_TENSOR
    states_total = jnp.zeros((grad_key.shape[0], DE), jnp.float32)
    for group in range(N_TENSOR):
        lower = group * width
        upper = lower + width
        piece = jnp.dot(grad_key[:, lower:upper], key_weight[:, lower:upper].T, preferred_element_type=jnp.float32) + jnp.dot(grad_value[:, lower:upper], value_weight[:, lower:upper].T, preferred_element_type=jnp.float32)
        states_total = states_total + piece.astype(jnp.bfloat16).astype(jnp.float32)
    grad_neighbours = states_total.astype(jnp.bfloat16).reshape(BLOCKS, NBR, DE)
    rows_out = (slot_target * NEED + block_ids[None, :]).reshape(-1).astype(jnp.int32)
    grad_states = jnp.take(grad_neighbours, rows_out, axis=0)
    return (cross_out, grad_hidden, grad_states)
```

```python
import functools
import math

import jax
import jax.numpy as jnp
from jax import lax
from jax.experimental import pallas as pl
from jax.experimental.pallas import tpu as pltpu
from jax.sharding import Mesh, PartitionSpec as P

HEAD = 128
SPAN = 64
NBR = 128
WINDOW = 4
DP = ("z", "x", "core")
VMEM_LIMIT = 56 * 1024 * 1024
F32, BF16 = jnp.float32, jnp.bfloat16

NN = (((1,), (0,)), ((), ()))
NT = (((1,), (1,)), ((), ()))
TN = (((0,), (0,)), ((), ()))


def dot(a, b, dims=NN):
    return lax.dot_general(a, b, dims, preferred_element_type=F32)


def params():
    return pltpu.CompilerParams(vmem_limit_bytes=VMEM_LIMIT)


def whole(shape):
    return pl.BlockSpec(shape, lambda *_: (0,) * len(shape))


def cost(flops, nbytes):
    return pl.CostEstimate(flops=int(flops), bytes_accessed=int(nbytes), transcendentals=0)


def from_peers(x):
    n = lax.axis_size("tensor")
    got = [x]
    for r in range(1, n):
        got.append(lax.ppermute(x, "tensor", [((i + r) % n, i) for i in range(n)]))
    return got


def to_peers(pieces):
    n = lax.axis_size("tensor")
    got = [pieces[0]]
    for r in range(1, n):
        got.append(lax.ppermute(pieces[r], "tensor", [(i, (i + r) % n) for i in range(n)]))
    return got


def summed(parts):
    total = parts[0].astype(F32)
    for part in parts[1:]:
        total = total + part.astype(F32)
    return total.astype(BF16)


def query_kernel(t_ref, h0, h1, h2, h3, w_ref, q_ref, acc):
    r = pl.program_id(0)
    for i, h in enumerate((h0, h1, h2, h3)):

        @pl.when(r == i)
        def _():
            part = dot(h[...], w_ref[...])
            if i == 0:
                acc[...] = part
            elif i < 3:
                acc[...] += part
            else:
                q_ref[...] = (acc[...] + part).astype(BF16)


def query_of(t, pieces, weight):
    rows, width = pieces[0].shape
    cols = weight.shape[1]
    return pl.pallas_call(
        query_kernel,
        out_shape=jax.ShapeDtypeStruct((rows, cols), BF16),
        grid_spec=pltpu.PrefetchScalarGridSpec(
            num_scalar_prefetch=1,
            grid=(4,),
            in_specs=[whole((rows, width))] * 4
            + [pl.BlockSpec((width, cols), lambda r, t: ((t[0] + r) % 4, 0))],
            out_specs=whole((rows, cols)),
            scratch_shapes=[pltpu.VMEM((rows, cols), F32)],
        ),
        compiler_params=params(),
        cost_estimate=cost(2 * rows * 4 * width * cols, 8 * width * cols),
        name="query",
    )(t, *pieces, weight)


def forward_kernel(
    scale, t_ref, q_ref, n0, n1, n2, n3, kw_ref, vw_ref, k_ref, v_ref, p_ref, a_ref, flipped, rows
):
    blocks, part, length = n0.shape

    @pl.when(pl.program_id(0) == 0)
    def _():
        for r, n in enumerate((n0, n1, n2, n3)):
            at = pl.multiple_of(((t_ref[0] + r) % 4) * part, part)
            for b in range(blocks):
                flipped[pl.ds(at, part), b * length : (b + 1) * length] = n[b]
        rows[...] = flipped[...].T

    k_ref[...] = dot(rows[...], kw_ref[...]).astype(BF16)
    v_ref[...] = dot(rows[...], vw_ref[...]).astype(BF16)
    spans = q_ref.shape[0] // SPAN
    keys = k_ref.shape[0] // spans
    for j in range(q_ref.shape[1] // HEAD):
        c = slice(j * HEAD, (j + 1) * HEAD)
        for s in range(spans):
            qs = slice(s * SPAN, (s + 1) * SPAN)
            ks = slice(s * keys, (s + 1) * keys)
            scores = dot(q_ref[qs, c], k_ref[ks, c], NT) * scale
            e = jnp.exp(scores - jnp.max(scores, axis=-1, keepdims=True))
            probs = e / jnp.sum(e, axis=-1, keepdims=True)
            p_ref[j, s] = probs
            a_ref[qs, c] = dot(probs.astype(BF16), v_ref[ks, c]).astype(BF16)


def forward_of(t, query, pieces, key_weight, value_weight):
    rows, cols = query.shape
    blocks, part, length = pieces[0].shape
    tokens, width = blocks * length, key_weight.shape[0]
    spans = rows // SPAN
    step = 2 * HEAD
    col = lambda n: pl.BlockSpec((n, step), lambda j, t: (0, j))
    return pl.pallas_call(
        functools.partial(forward_kernel, 1.0 / math.sqrt(HEAD)),
        out_shape=(
            jax.ShapeDtypeStruct((tokens, cols), BF16),
            jax.ShapeDtypeStruct((tokens, cols), BF16),
            jax.ShapeDtypeStruct((cols // HEAD, spans, SPAN, tokens // spans), F32),
            jax.ShapeDtypeStruct((rows, cols), BF16),
        ),
        grid_spec=pltpu.PrefetchScalarGridSpec(
            num_scalar_prefetch=1,
            grid=(cols // step,),
            in_specs=[col(rows)] + [whole(pieces[0].shape)] * 4 + [col(width)] * 2,
            out_specs=[
                col(tokens),
                col(tokens),
                pl.BlockSpec((2, spans, SPAN, tokens // spans), lambda j, t: (j, 0, 0, 0)),
                col(rows),
            ],
            scratch_shapes=[pltpu.VMEM((width, tokens), BF16), pltpu.VMEM((tokens, width), BF16)],
        ),
        compiler_params=params(),
        cost_estimate=cost(4 * tokens * width * cols, 10e6),
        name="forward",
    )(t, query, *pieces, key_weight, value_weight)


def output_kernel(t_ref, a_ref, g0, g1, g2, g3, w_ref, o0, o1, o2, o3, ga_ref, acc):
    r = pl.program_id(0)
    for i, (g, o) in enumerate(((g0, o0), (g1, o1), (g2, o2), (g3, o3))):

        @pl.when(r == i)
        def _():
            w = w_ref[...]
            part = dot(g[...], w)
            o[...] = dot(a_ref[...], w, NT).astype(BF16)
            if i == 0:
                acc[...] = part
            elif i < 3:
                acc[...] += part
            else:
                ga_ref[...] = (acc[...] + part).astype(BF16)


def output_of(t, attended, pieces, weight):
    rows, width = pieces[0].shape
    cols = weight.shape[1]
    return pl.pallas_call(
        output_kernel,
        out_shape=[jax.ShapeDtypeStruct((rows, width), BF16)] * 4
        + [jax.ShapeDtypeStruct((rows, cols), BF16)],
        grid_spec=pltpu.PrefetchScalarGridSpec(
            num_scalar_prefetch=1,
            grid=(4,),
            in_specs=[whole((rows, cols))]
            + [whole((rows, width))] * 4
            + [pl.BlockSpec((width, cols), lambda r, t: ((t[0] + r) % 4, 0))],
            out_specs=[whole((rows, width))] * 4 + [whole((rows, cols))],
            scratch_shapes=[pltpu.VMEM((rows, cols), F32)],
        ),
        compiler_params=params(),
        cost_estimate=cost(4 * rows * 4 * width * cols, 8 * width * cols),
        name="output",
    )(t, attended, *pieces, weight)


def backward_kernel(
    scale, t_ref, ga_ref, q_ref, k_ref, v_ref, p_ref, kw_ref, vw_ref, gq_ref, s0, s1, s2, s3, gk, gv, acc
):
    j, last = pl.program_id(0), pl.num_programs(0) - 1
    spans = q_ref.shape[0] // SPAN
    keys = k_ref.shape[0] // spans
    for h in range(q_ref.shape[1] // HEAD):
        c = slice(h * HEAD, (h + 1) * HEAD)
        for s in range(spans):
            qs = slice(s * SPAN, (s + 1) * SPAN)
            ks = slice(s * keys, (s + 1) * keys)
            probs, ga = p_ref[h, s], ga_ref[qs, c]
            gp = dot(ga, v_ref[ks, c], NT)
            inner = jnp.sum(probs * gp, axis=-1, keepdims=True)
            gs = (probs * (gp - inner) * scale).astype(BF16)
            gq_ref[qs, c] = dot(gs, k_ref[ks, c]).astype(BF16)
            gk[ks, c] = dot(gs, q_ref[qs, c], TN).astype(BF16)
            gv[ks, c] = dot(probs.astype(BF16), ga, TN).astype(BF16)
    part = dot(kw_ref[...], gk[...], NT) + dot(vw_ref[...], gv[...], NT)

    @pl.when(j == 0)
    def _():
        acc[...] = part

    @pl.when(j > 0)
    def _():
        acc[...] += part

    @pl.when(j == last)
    def _():
        blocks, rows, length = s0.shape
        for r, out in enumerate((s0, s1, s2, s3)):
            at = pl.multiple_of(((t_ref[0] + r) % 4) * rows, rows)
            for b in range(blocks):
                out[b] = acc[pl.ds(at, rows), b * length : (b + 1) * length].astype(BF16)


def backward_of(t, ga, query, key, value, probs, key_weight, value_weight, piece):
    rows, cols = query.shape
    tokens, width = key.shape[0], key_weight.shape[0]
    spans = rows // SPAN
    step = 2 * HEAD
    col = lambda n: pl.BlockSpec((n, step), lambda j, t: (0, j))
    return pl.pallas_call(
        functools.partial(backward_kernel, 1.0 / math.sqrt(HEAD)),
        out_shape=[jax.ShapeDtypeStruct((rows, cols), BF16)] + [jax.ShapeDtypeStruct(piece, BF16)] * 4,
        grid_spec=pltpu.PrefetchScalarGridSpec(
            num_scalar_prefetch=1,
            grid=(cols // step,),
            in_specs=[
                col(rows),
                col(rows),
                col(tokens),
                col(tokens),
                pl.BlockSpec((2, spans, SPAN, tokens // spans), lambda j, t: (j, 0, 0, 0)),
                col(width),
                col(width),
            ],
            out_specs=[col(rows)] + [whole(piece)] * 4,
            scratch_shapes=[
                pltpu.VMEM((tokens, step), BF16),
                pltpu.VMEM((tokens, step), BF16),
                pltpu.VMEM((width, tokens), F32),
            ],
        ),
        compiler_params=params(),
        cost_estimate=cost(4 * tokens * width * cols, 10e6),
        name="backward",
    )(t, ga, query, key, value, probs, key_weight, value_weight)


def hidden_kernel(t_ref, g_ref, w_ref, o0, o1, o2, o3):
    r = pl.program_id(0)
    for i, o in enumerate((o0, o1, o2, o3)):

        @pl.when(r == i)
        def _():
            o[...] = dot(g_ref[...], w_ref[...], NT).astype(BF16)


def hidden_of(t, grad_query, weight):
    rows, cols = grad_query.shape
    width = weight.shape[0] // 4
    return pl.pallas_call(
        hidden_kernel,
        out_shape=[jax.ShapeDtypeStruct((rows, width), BF16)] * 4,
        grid_spec=pltpu.PrefetchScalarGridSpec(
            num_scalar_prefetch=1,
            grid=(4,),
            in_specs=[
                whole((rows, cols)),
                pl.BlockSpec((width, cols), lambda r, t: ((t[0] + r) % 4, 0)),
            ],
            out_specs=[whole((rows, width))] * 4,
        ),
        compiler_params=params(),
        cost_estimate=cost(2 * rows * 4 * width * cols, 8 * width * cols),
        name="hidden",
    )(t, grad_query, weight)


def pairs_moved(first, second, gaps, sign):
    n = math.prod(lax.axis_size(a) for a in DP)

    def moved(x, by):
        return lax.ppermute(x, DP, [(i, (i + sign * by) % n) for i in range(n)])

    def branch(index):
        return lambda a, b: (moved(a, index // WINDOW + 1), moved(b, index % WINDOW + 1))

    which = (gaps[0] - 1) * WINDOW + gaps[1] - 1
    return lax.switch(which, [branch(i) for i in range(WINDOW * WINDOW)], first, second)


def shards(
    hidden,
    grad_out,
    query_weight,
    key_weight,
    value_weight,
    out_weight,
    neighbour_states,
    block_owner,
    slot_target,
):
    n_dp = math.prod(lax.axis_size(a) for a in DP)
    t = lax.axis_index("tensor").astype(jnp.int32).reshape(1)
    out_full = lax.all_gather(out_weight.T, DP, axis=0, tiled=True)

    gap = (block_owner[0] - lax.axis_index(DP) + n_dp) % n_dp
    gaps = (gap[0], gap[2])
    states = jnp.swapaxes(neighbour_states, 1, 2)
    first, second = pairs_moved(states[:2], states[2:], gaps, -1)
    mine = jnp.concatenate([first, second], axis=0)

    hidden_pieces = from_peers(hidden)
    neighbours = from_peers(mine)
    grad_pieces = from_peers(grad_out)

    query = query_of(t, hidden_pieces, query_weight)
    key, value, probs, attended = forward_of(t, query, neighbours, key_weight, value_weight)
    *out_parts, grad_attended = output_of(t, attended, grad_pieces, out_full)
    cross_out = summed(to_peers(out_parts))
    grad_query, *state_parts = backward_of(
        t, grad_attended, query, key, value, probs, key_weight, value_weight, mine.shape
    )
    grads = summed(to_peers(state_parts))
    grad_hidden = summed(to_peers(hidden_of(t, grad_query, query_weight)))
    first, second = pairs_moved(grads[:2], grads[2:], gaps, 1)
    grad_states = jnp.swapaxes(jnp.concatenate([first, second], axis=0), 1, 2)
    return cross_out, grad_hidden, grad_states


def solution(mesh):
    grid = Mesh(mesh.devices.reshape(8, 4, 2, 4), DP + ("tensor",))
    placed = (
        P(DP, "tensor"),
        P(DP, "tensor"),
        P(None, "tensor"),
        P(None, "tensor"),
        P(None, "tensor"),
        P("tensor", DP),
        P(DP, None, "tensor"),
        P(DP, None),
        P(DP, None),
    )
    return jax.shard_map(
        shards,
        mesh=grid,
        in_specs=placed,
        out_specs=(P(DP, "tensor"), P(DP, "tensor"), P(DP, None, "tensor")),
        check_vma=False,
    )
```

```python
import functools
import math

import jax
import jax.numpy as jnp
from jax import lax
from jax.experimental import pallas as pl
from jax.experimental.pallas import tpu as pltpu
from jax.sharding import Mesh, PartitionSpec as P

HEAD = 128
SPAN = 64
NBR = 128
WINDOW = 4
DP = ("z", "x", "core")
MIB = 1024 * 1024
F32, BF16 = jnp.float32, jnp.bfloat16

NN = (((1,), (0,)), ((), ()))
NT = (((1,), (1,)), ((), ()))
TN = (((0,), (0,)), ((), ()))


def dot(a, b, dims=NN):
    return lax.dot_general(a, b, dims, preferred_element_type=F32)


def params(mib):
    return pltpu.CompilerParams(vmem_limit_bytes=mib * MIB)


ANY = pl.BlockSpec(memory_space=pl.ANY)


def whole(shape):
    return pl.BlockSpec(shape, lambda *_: (0,) * len(shape))


def cost(flops, nbytes):
    return pl.CostEstimate(flops=int(flops), bytes_accessed=int(nbytes), transcendentals=0)


def from_peers(x):
    n = lax.axis_size("tensor")
    got = [x]
    for r in range(1, n):
        got.append(lax.ppermute(x, "tensor", [((i + r) % n, i) for i in range(n)]))
    return got


def to_peers(pieces):
    n = lax.axis_size("tensor")
    got = [pieces[0]]
    for r in range(1, n):
        got.append(lax.ppermute(pieces[r], "tensor", [(i, (i + r) % n) for i in range(n)]))
    return got


def swapped(x):
    return lax.ppermute(x, "core", [(0, 1), (1, 0)])


def summed(parts):
    total = parts[0].astype(F32)
    for part in parts[1:]:
        total = total + part.astype(F32)
    return total.astype(BF16)


def query_kernel(t_ref, h0, h1, h2, h3, w_ref, q_ref, acc):
    r = pl.program_id(0)
    for i, h in enumerate((h0, h1, h2, h3)):

        @pl.when(r == i)
        def _():
            part = dot(h[...], w_ref[...])
            if i == 0:
                acc[...] = part
            elif i < 3:
                acc[...] += part
            else:
                q_ref[...] = (acc[...] + part).astype(BF16)


def query_of(t, pieces, weight):
    rows, width = pieces[0].shape
    cols = weight.shape[1]
    return pl.pallas_call(
        query_kernel,
        out_shape=jax.ShapeDtypeStruct((rows, cols), BF16),
        grid_spec=pltpu.PrefetchScalarGridSpec(
            num_scalar_prefetch=1,
            grid=(4,),
            in_specs=[whole((rows, width))] * 4
            + [pl.BlockSpec((width, cols), lambda r, t: ((t[0] + r) % 4, 0))],
            out_specs=whole((rows, cols)),
            scratch_shapes=[pltpu.VMEM((rows, cols), F32)],
        ),
        compiler_params=params(56),
        cost_estimate=cost(2 * rows * 4 * width * cols, 8 * width * cols),
        name="query",
    )(t, *pieces, weight)


def forward_kernel(
    scale, t_ref, q_ref, n0, n1, n2, n3, kw_ref, vw_ref, k_ref, v_ref, p_ref, a_own, a_other, flipped, rows
):
    blocks, part, length = n0.shape

    @pl.when(pl.program_id(0) == 0)
    def _():
        for r, n in enumerate((n0, n1, n2, n3)):
            at = pl.multiple_of(((t_ref[0] + r) % 4) * part, part)
            for b in range(blocks):
                flipped[pl.ds(at, part), b * length : (b + 1) * length] = n[b]
        rows[...] = flipped[...].T

    k_ref[...] = dot(rows[...], kw_ref[...]).astype(BF16)
    v_ref[...] = dot(rows[...], vw_ref[...]).astype(BF16)
    spans = q_ref.shape[0] // SPAN
    keys = k_ref.shape[0] // spans
    step, half = pl.program_id(0), pl.num_programs(0) // 2
    attended = []
    for j in range(q_ref.shape[1] // HEAD):
        c = slice(j * HEAD, (j + 1) * HEAD)
        for s in range(spans):
            qs = slice(s * SPAN, (s + 1) * SPAN)
            ks = slice(s * keys, (s + 1) * keys)
            scores = dot(q_ref[qs, c], k_ref[ks, c], NT) * scale
            e = jnp.exp(scores - jnp.max(scores, axis=-1, keepdims=True))
            probs = e / jnp.sum(e, axis=-1, keepdims=True)
            p_ref[j, s] = probs
            attended.append((qs, j * HEAD, dot(probs.astype(BF16), v_ref[ks, c]).astype(BF16)))
    first = (step % half) * q_ref.shape[1]
    mine = step // half == t_ref[1]

    def keep(out):
        for qs, at, value in attended:
            out[qs, pl.ds(pl.multiple_of(first + at, HEAD), HEAD)] = value

    @pl.when(mine)
    def _():
        keep(a_own)

    @pl.when(jnp.logical_not(mine))
    def _():
        keep(a_other)


def forward_of(t, query, pieces, key_weight, value_weight):
    rows, cols = query.shape
    blocks, part, length = pieces[0].shape
    tokens, width = blocks * length, key_weight.shape[0]
    spans = rows // SPAN
    step = 2 * HEAD
    col = lambda n: pl.BlockSpec((n, step), lambda j, t: (0, j))
    return pl.pallas_call(
        functools.partial(forward_kernel, 1.0 / math.sqrt(HEAD)),
        out_shape=(
            jax.ShapeDtypeStruct((tokens, cols), BF16),
            jax.ShapeDtypeStruct((tokens, cols), BF16),
            jax.ShapeDtypeStruct((cols // HEAD, spans, SPAN, tokens // spans), F32),
            jax.ShapeDtypeStruct((rows, cols // 2), BF16),
            jax.ShapeDtypeStruct((rows, cols // 2), BF16),
        ),
        grid_spec=pltpu.PrefetchScalarGridSpec(
            num_scalar_prefetch=1,
            grid=(cols // step,),
            in_specs=[col(rows)] + [whole(pieces[0].shape)] * 4 + [col(width)] * 2,
            out_specs=[
                col(tokens),
                col(tokens),
                pl.BlockSpec((2, spans, SPAN, tokens // spans), lambda j, t: (j, 0, 0, 0)),
                whole((rows, cols // 2)),
                whole((rows, cols // 2)),
            ],
            scratch_shapes=[pltpu.VMEM((width, tokens), BF16), pltpu.VMEM((tokens, width), BF16)],
        ),
        compiler_params=params(56),
        cost_estimate=cost(4 * tokens * width * cols, 10e6),
        name="forward",
    )(t, query, *pieces, key_weight, value_weight)


def grad_attended_kernel(t_ref, *refs):
    own, other, w_ref, ga_own, ga_other, acc = refs[:4], refs[4:8], *refs[8:]
    r = pl.program_id(0)
    rows = ga_own.shape[0]
    for i in range(4):

        @pl.when(r == i)
        def _():
            part = dot(jnp.concatenate([own[i][...], other[i][...]], axis=0), w_ref[...])
            if i == 0:
                acc[...] = part
            elif i < 3:
                acc[...] += part
            else:
                total = (acc[...] + part).astype(BF16)
                ga_own[...] = total[:rows]
                ga_other[...] = total[rows:]


def grad_attended_of(t, own, other, weight):
    rows, width = own[0].shape
    cols = weight.shape[1]
    return pl.pallas_call(
        grad_attended_kernel,
        out_shape=[jax.ShapeDtypeStruct((rows, cols), BF16)] * 2,
        grid_spec=pltpu.PrefetchScalarGridSpec(
            num_scalar_prefetch=1,
            grid=(4,),
            in_specs=[whole((rows, width))] * 8
            + [pl.BlockSpec((width, cols), lambda r, t: ((t[0] + r) % 4, 0))],
            out_specs=[whole((rows, cols))] * 2,
            scratch_shapes=[pltpu.VMEM((2 * rows, cols), F32)],
        ),
        compiler_params=params(56),
        cost_estimate=cost(4 * rows * 4 * width * cols, 8 * width * cols),
        name="grad_attended",
    )(t, *own, *other, weight)


def output_kernel(t_ref, own_ref, other_ref, w_ref, _, o_own, o_other):
    rows = own_ref.shape[0]
    both = jnp.concatenate([own_ref[...], other_ref[...]], axis=0)
    out = dot(both, w_ref[...], NT).astype(BF16)
    o_own[0] = out[:rows]
    o_other[0] = out[rows:]


def output_of(t, own, other, weight, after):
    rows, cols = own.shape
    width = weight.shape[0] // 4
    return pl.pallas_call(
        output_kernel,
        out_shape=[jax.ShapeDtypeStruct((4, rows, width), BF16)] * 2,
        grid_spec=pltpu.PrefetchScalarGridSpec(
            num_scalar_prefetch=1,
            grid=(4,),
            in_specs=[whole((rows, cols))] * 2
            + [pl.BlockSpec((width, cols), lambda r, t: ((t[0] + r) % 4, 0)), ANY],
            out_specs=[pl.BlockSpec((1, rows, width), lambda r, t: (r, 0, 0))] * 2,
        ),
        compiler_params=params(56),
        cost_estimate=cost(4 * rows * 4 * width * cols, 8 * width * cols),
        name="output",
    )(t, own, other, weight, after)


def backward_kernel(scale, final, t_ref, ga_ref, q_ref, k_ref, v_ref, p_ref, kw_ref, vw_ref, before, _, *refs):
    gq_ref, outs, (gk, gv, acc) = refs[0], refs[1:-3], refs[-3:]
    j, last = pl.program_id(0), pl.num_programs(0) - 1
    spans = q_ref.shape[0] // SPAN
    keys = k_ref.shape[0] // spans
    for h in range(q_ref.shape[1] // HEAD):
        c = slice(h * HEAD, (h + 1) * HEAD)
        for s in range(spans):
            qs = slice(s * SPAN, (s + 1) * SPAN)
            ks = slice(s * keys, (s + 1) * keys)
            probs, ga = p_ref[h, s], ga_ref[qs, c]
            gp = dot(ga, v_ref[ks, c], NT)
            inner = jnp.sum(probs * gp, axis=-1, keepdims=True)
            gs = (probs * (gp - inner) * scale).astype(BF16)
            gq_ref[qs, c] = dot(gs, k_ref[ks, c]).astype(BF16)
            gk[ks, c] = dot(gs, q_ref[qs, c], TN).astype(BF16)
            gv[ks, c] = dot(probs.astype(BF16), ga, TN).astype(BF16)
    part = dot(kw_ref[...], gk[...], NT) + dot(vw_ref[...], gv[...], NT)

    @pl.when(j == 0)
    def _():
        acc[...] = before[...] + part if final else part

    @pl.when(j > 0)
    def _():
        acc[...] += part

    @pl.when(j == last)
    def _():
        if not final:
            outs[0][...] = acc[...]
            return
        blocks, rows, length = outs[0].shape
        for r, out in enumerate(outs):
            at = pl.multiple_of(((t_ref[0] + r) % 4) * rows, rows)
            for b in range(blocks):
                out[b] = acc[pl.ds(at, rows), b * length : (b + 1) * length].astype(BF16)


def backward_of(t, ga, query, key, value, probs, key_weight, value_weight, before, after, piece=None):
    rows, cols = ga.shape
    tokens, width = key.shape[0], key_weight.shape[0]
    spans = rows // SPAN
    step = 2 * HEAD
    steps = cols // step
    final = piece is not None

    def at(j, t):
        return (1 - t[1] if final else t[1]) * steps + j

    col = lambda n: pl.BlockSpec((n, step), lambda j, t: (0, at(j, t)))
    here = pl.BlockSpec((rows, step), lambda j, t: (0, j))
    state = jax.ShapeDtypeStruct((width, tokens), F32)
    outs = [jax.ShapeDtypeStruct(piece, BF16)] * 4 if final else [state]
    return pl.pallas_call(
        functools.partial(backward_kernel, 1.0 / math.sqrt(HEAD), final),
        out_shape=[jax.ShapeDtypeStruct((rows, cols), BF16)] + outs,
        grid_spec=pltpu.PrefetchScalarGridSpec(
            num_scalar_prefetch=1,
            grid=(steps,),
            in_specs=[
                here,
                col(rows),
                col(tokens),
                col(tokens),
                pl.BlockSpec((2, spans, SPAN, tokens // spans), lambda j, t: (at(j, t), 0, 0, 0)),
                col(width),
                col(width),
                whole((width, tokens)) if final else ANY,
                ANY,
            ],
            out_specs=[here] + [whole(o.shape) for o in outs],
            scratch_shapes=[
                pltpu.VMEM((tokens, step), BF16),
                pltpu.VMEM((tokens, step), BF16),
                pltpu.VMEM((width, tokens), F32),
            ],
        ),
        compiler_params=params(56),
        cost_estimate=cost(4 * tokens * width * cols, 5e6),
        name="backward",
    )(t, ga, query, key, value, probs, key_weight, value_weight, before, after)


def hidden_kernel(t_ref, own_ref, other_ref, w_own, w_other, o0, o1, o2, o3):
    r = pl.program_id(0)
    for i, o in enumerate((o0, o1, o2, o3)):

        @pl.when(r == i)
        def _():
            o[...] = (dot(own_ref[...], w_own[...], NT) + dot(other_ref[...], w_other[...], NT)).astype(BF16)


def hidden_of(t, own, other, weight):
    rows, cols = own.shape
    width = weight.shape[0] // 4
    return pl.pallas_call(
        hidden_kernel,
        out_shape=[jax.ShapeDtypeStruct((rows, width), BF16)] * 4,
        grid_spec=pltpu.PrefetchScalarGridSpec(
            num_scalar_prefetch=1,
            grid=(4,),
            in_specs=[
                whole((rows, cols)),
                whole((rows, cols)),
                pl.BlockSpec((width, cols), lambda r, t: ((t[0] + r) % 4, t[1])),
                pl.BlockSpec((width, cols), lambda r, t: ((t[0] + r) % 4, 1 - t[1])),
            ],
            out_specs=[whole((rows, width))] * 4,
        ),
        compiler_params=params(56),
        cost_estimate=cost(4 * rows * 4 * width * cols, 16 * width * cols),
        name="hidden",
    )(t, own, other, weight, weight)


def pairs_moved(first, second, gaps, sign):
    n = math.prod(lax.axis_size(a) for a in DP)

    def moved(x, by):
        return lax.ppermute(x, DP, [(i, (i + sign * by) % n) for i in range(n)])

    def branch(index):
        return lambda a, b: (moved(a, index // WINDOW + 1), moved(b, index % WINDOW + 1))

    which = (gaps[0] - 1) * WINDOW + gaps[1] - 1
    return lax.switch(which, [branch(i) for i in range(WINDOW * WINDOW)], first, second)


def delivered(states, gaps):
    n = math.prod(lax.axis_size(a) for a in DP)
    pairs = states[:2], states[2:]
    got = [None, None]
    for by in range(1, WINDOW + 1):
        sent = jnp.where(gaps[0] == by, *pairs)
        came = lax.ppermute(sent, DP, [(i, (i - by) % n) for i in range(n)])
        got = [came if g is None else jnp.where(gaps[k] == by, came, g) for k, g in enumerate(got)]
    return jnp.concatenate(got, axis=0)


def gathered_half(rows):
    half = rows.shape[1] // 2
    chips, cores = lax.axis_size("x"), lax.axis_size("core")
    halves = jnp.stack([rows[:, :half], rows[:, half:]], axis=0)
    sent = jnp.broadcast_to(halves, (chips, *halves.shape)).reshape(chips * cores, *halves.shape[1:])
    plane = lax.all_to_all(sent, ("x", "core"), split_axis=0, concat_axis=0, tiled=True)
    return lax.all_gather(plane.reshape(-1, half), "z", axis=0, tiled=True)


def shards(
    hidden,
    grad_out,
    query_weight,
    key_weight,
    value_weight,
    out_weight,
    neighbour_states,
    block_owner,
    slot_target,
):
    n_dp = math.prod(lax.axis_size(a) for a in DP)
    core = lax.axis_index("core")
    t = jnp.stack([lax.axis_index("tensor"), core]).astype(jnp.int32)
    out_own = gathered_half(out_weight.T)

    gap = (block_owner[0] - lax.axis_index(DP) + n_dp) % n_dp
    gaps = (gap[0], gap[2])
    hidden_pieces = from_peers(hidden)
    mine = delivered(jnp.swapaxes(neighbour_states, 1, 2), gaps)
    neighbours = from_peers(mine)
    grad_pieces = from_peers(grad_out)
    grad_others = [swapped(g) for g in grad_pieces]

    query = query_of(t, hidden_pieces, query_weight)
    key, value, probs, attended, lent = forward_of(t, query, neighbours, key_weight, value_weight)
    ga_own, ga_lent = grad_attended_of(t, grad_pieces, grad_others, out_own)
    ga_other = swapped(ga_lent)
    out_parts, out_lent = output_of(t, attended, swapped(lent), out_own, ga_own)
    out_back = swapped(out_lent)
    context = query, key, value, probs, key_weight, value_weight
    gq_own, states_half = backward_of(t, ga_own, *context, out_parts, out_lent)
    out_pieces = [summed([out_parts[r], out_back[r]]) for r in range(4)]
    gq_other, *state_parts = backward_of(
        t, ga_other, *context, states_half, out_pieces[1], mine.shape
    )
    cross_out = summed(to_peers(out_pieces))
    grads = summed(to_peers(state_parts))
    grad_hidden = summed(to_peers(hidden_of(t, gq_own, gq_other, query_weight)))
    first, second = pairs_moved(grads[:2], grads[2:], gaps, 1)
    grad_states = jnp.swapaxes(jnp.concatenate([first, second], axis=0), 1, 2)
    return cross_out, grad_hidden, grad_states


def solution(mesh):
    grid = Mesh(mesh.devices.reshape(8, 4, 2, 4), DP + ("tensor",))
    placed = (
        P(DP, "tensor"),
        P(DP, "tensor"),
        P(None, "tensor"),
        P(None, "tensor"),
        P(None, "tensor"),
        P("tensor", DP),
        P(DP, None, "tensor"),
        P(DP, None),
        P(DP, None),
    )
    return jax.shard_map(
        shards,
        mesh=grid,
        in_specs=placed,
        out_specs=(P(DP, "tensor"), P(DP, "tensor"), P(DP, None, "tensor")),
        check_vma=False,
    )
```

```python
import functools
import math

import jax
import jax.numpy as jnp
from jax import lax
from jax.experimental import pallas as pl
from jax.experimental.pallas import tpu as pltpu
from jax.sharding import Mesh, PartitionSpec as P

HEAD = 128
SPAN = 64
NBR = 128
WINDOW = 4
DP = ("z", "x", "core")
MIB = 1024 * 1024
F32, BF16 = jnp.float32, jnp.bfloat16

NN = (((1,), (0,)), ((), ()))
NT = (((1,), (1,)), ((), ()))
TN = (((0,), (0,)), ((), ()))


def dot(a, b, dims=NN):
    return lax.dot_general(a, b, dims, preferred_element_type=F32)


def params(mib):
    return pltpu.CompilerParams(vmem_limit_bytes=mib * MIB)


ANY = pl.BlockSpec(memory_space=pl.ANY)
VMEM = pl.BlockSpec(memory_space=pltpu.VMEM)
HBM = pl.BlockSpec(memory_space=pltpu.HBM)
SMEM = pl.BlockSpec(memory_space=pltpu.SMEM)


def whole(shape):
    return pl.BlockSpec(shape, lambda *_: (0,) * len(shape))


def cost(flops, nbytes):
    return pl.CostEstimate(flops=int(flops), bytes_accessed=int(nbytes), transcendentals=0)


def from_peers(x):
    n = lax.axis_size("tensor")
    got = [x]
    for r in range(1, n):
        got.append(lax.ppermute(x, "tensor", [((i + r) % n, i) for i in range(n)]))
    return got


def to_peers(pieces):
    n = lax.axis_size("tensor")
    got = [pieces[0]]
    for r in range(1, n):
        got.append(lax.ppermute(pieces[r], "tensor", [(i, (i + r) % n) for i in range(n)]))
    return got


def summed(parts):
    total = parts[0].astype(F32)
    for part in parts[1:]:
        total = total + part.astype(F32)
    return total.astype(BF16)


def nothing(*_):
    pass


def tied(x, *after):
    return pl.pallas_call(
        nothing,
        out_shape=jax.ShapeDtypeStruct(x.shape, x.dtype),
        in_specs=[ANY] * (1 + len(after)),
        out_specs=ANY,
        input_output_aliases={0: 0},
        name="tied",
    )(x, *after)


def query_kernel(t_ref, h0, h1, h2, h3, w_ref, q_ref, acc):
    r = pl.program_id(0)
    for i, h in enumerate((h0, h1, h2, h3)):

        @pl.when(r == i)
        def _():
            part = dot(h[...], w_ref[...])
            if i == 0:
                acc[...] = part
            elif i < 3:
                acc[...] += part
            else:
                q_ref[...] = (acc[...] + part).astype(BF16)


def query_of(t, pieces, weight):
    rows, width = pieces[0].shape
    cols = weight.shape[1]
    return pl.pallas_call(
        query_kernel,
        out_shape=jax.ShapeDtypeStruct((rows, cols), BF16),
        grid_spec=pltpu.PrefetchScalarGridSpec(
            num_scalar_prefetch=1,
            grid=(4,),
            in_specs=[whole((rows, width))] * 4
            + [pl.BlockSpec((width, cols), lambda r, t: ((t[0] + r) % 4, 0))],
            out_specs=whole((rows, cols)),
            scratch_shapes=[pltpu.VMEM((rows, cols), F32)],
        ),
        compiler_params=params(56),
        cost_estimate=cost(2 * rows * 4 * width * cols, 8 * width * cols),
        name="query",
    )(t, *pieces, weight)


def forward_kernel(
    scale, t_ref, q_ref, n0, n1, n2, n3, kw_ref, vw_ref, k_ref, v_ref, p_ref, a_ref, flipped, rows
):
    blocks, part, length = n0.shape

    @pl.when(pl.program_id(0) == 0)
    def _():
        for r, n in enumerate((n0, n1, n2, n3)):
            at = pl.multiple_of(((t_ref[0] + r) % 4) * part, part)
            for b in range(blocks):
                flipped[pl.ds(at, part), b * length : (b + 1) * length] = n[b]
        rows[...] = flipped[...].T

    k_ref[...] = dot(rows[...], kw_ref[...]).astype(BF16)
    v_ref[...] = dot(rows[...], vw_ref[...]).astype(BF16)
    spans = q_ref.shape[0] // SPAN
    keys = k_ref.shape[0] // spans
    for j in range(q_ref.shape[1] // HEAD):
        c = slice(j * HEAD, (j + 1) * HEAD)
        for s in range(spans):
            qs = slice(s * SPAN, (s + 1) * SPAN)
            ks = slice(s * keys, (s + 1) * keys)
            scores = dot(q_ref[qs, c], k_ref[ks, c], NT) * scale
            e = jnp.exp(scores - jnp.max(scores, axis=-1, keepdims=True))
            probs = e / jnp.sum(e, axis=-1, keepdims=True)
            p_ref[j, s] = probs
            a_ref[qs, c] = dot(probs.astype(BF16), v_ref[ks, c]).astype(BF16)


def forward_of(t, query, pieces, key_weight, value_weight):
    rows, cols = query.shape
    blocks, part, length = pieces[0].shape
    tokens, width = blocks * length, key_weight.shape[0]
    spans = rows // SPAN
    step = 2 * HEAD
    col = lambda n: pl.BlockSpec((n, step), lambda j, t: (0, j))
    return pl.pallas_call(
        functools.partial(forward_kernel, 1.0 / math.sqrt(HEAD)),
        out_shape=(
            jax.ShapeDtypeStruct((tokens, cols), BF16),
            jax.ShapeDtypeStruct((tokens, cols), BF16),
            jax.ShapeDtypeStruct((cols // HEAD, spans, SPAN, tokens // spans), F32),
            jax.ShapeDtypeStruct((rows, cols), BF16),
        ),
        grid_spec=pltpu.PrefetchScalarGridSpec(
            num_scalar_prefetch=1,
            grid=(cols // step,),
            in_specs=[col(rows)] + [whole(pieces[0].shape)] * 4 + [col(width)] * 2,
            out_specs=[
                col(tokens),
                col(tokens),
                pl.BlockSpec((2, spans, SPAN, tokens // spans), lambda j, t: (j, 0, 0, 0)),
                col(rows),
            ],
            scratch_shapes=[pltpu.VMEM((width, tokens), BF16), pltpu.VMEM((tokens, width), BF16)],
        ),
        compiler_params=params(56),
        cost_estimate=cost(4 * tokens * width * cols, 10e6),
        name="forward",
    )(t, query, *pieces, key_weight, value_weight)


def output_kernel(t_ref, a_ref, g0, g1, g2, g3, own, other, o_ref, ga_ref, w_ref, sems):
    t, core, x = t_ref[0], t_ref[1], t_ref[2]
    steps, chips = 4, own.shape[1]
    deep = own.shape[0] // steps
    rows, width = g0.shape
    copies = []
    for r in range(steps):
        z = ((t + r) % steps) * deep
        for s in range(chips):
            at = (x - s + chips) % chips
            for n, (plane, c) in enumerate(((own, core), (other, 1 - core))):
                copies.append(
                    pltpu.make_async_copy(
                        plane.at[pl.ds(z, deep), s], w_ref.at[r, :, at, c], sems.at[r, 2 * s + n]
                    )
                )
    for copy in copies:
        copy.start()
    total = None
    for r, g in enumerate((g0, g1, g2, g3)):
        for copy in copies[r * 2 * chips : (r + 1) * 2 * chips]:
            copy.wait()
        w = w_ref[r].reshape(width, a_ref.shape[1])
        part = dot(g[...], w)
        total = part if total is None else total + part
        o_ref[(t + r) % steps] = dot(a_ref[...], w, NT).astype(BF16)
    ga_ref[...] = total.astype(BF16)


def output_of(t, attended, pieces, own, other):
    rows, width = pieces[0].shape
    cols = attended.shape[1]
    deep, chips = own.shape[0] // 4, own.shape[1]
    return pl.pallas_call(
        output_kernel,
        out_shape=(
            jax.ShapeDtypeStruct((4, rows, width), BF16),
            jax.ShapeDtypeStruct((rows, cols), BF16),
        ),
        in_specs=[SMEM] + [VMEM] * 5 + [HBM, ANY],
        out_specs=(VMEM, VMEM),
        scratch_shapes=[
            pltpu.VMEM((4, deep, chips, 2, *own.shape[2:]), BF16),
            pltpu.SemaphoreType.DMA((4, 2 * chips)),
        ],
        compiler_params=params(28),
        cost_estimate=cost(4 * rows * 4 * width * cols, 8 * width * cols),
        name="output",
    )(t, attended, *pieces, own, other)


def backward_kernel(
    scale, t_ref, ga_ref, q_ref, k_ref, v_ref, p_ref, kw_ref, vw_ref, gq_ref, s0, s1, s2, s3, gk, gv, acc
):
    j, last = pl.program_id(0), pl.num_programs(0) - 1
    spans = q_ref.shape[0] // SPAN
    keys = k_ref.shape[0] // spans
    for h in range(q_ref.shape[1] // HEAD):
        c = slice(h * HEAD, (h + 1) * HEAD)
        for s in range(spans):
            qs = slice(s * SPAN, (s + 1) * SPAN)
            ks = slice(s * keys, (s + 1) * keys)
            probs, ga = p_ref[h, s], ga_ref[qs, c]
            gp = dot(ga, v_ref[ks, c], NT)
            inner = jnp.sum(probs * gp, axis=-1, keepdims=True)
            gs = (probs * (gp - inner) * scale).astype(BF16)
            gq_ref[qs, c] = dot(gs, k_ref[ks, c]).astype(BF16)
            gk[ks, c] = dot(gs, q_ref[qs, c], TN).astype(BF16)
            gv[ks, c] = dot(probs.astype(BF16), ga, TN).astype(BF16)
    part = dot(kw_ref[...], gk[...], NT) + dot(vw_ref[...], gv[...], NT)

    @pl.when(j == 0)
    def _():
        acc[...] = part

    @pl.when(j > 0)
    def _():
        acc[...] += part

    @pl.when(j == last)
    def _():
        blocks, rows, length = s0.shape
        for r, out in enumerate((s0, s1, s2, s3)):
            at = pl.multiple_of(((t_ref[0] + r) % 4) * rows, rows)
            for b in range(blocks):
                out[b] = acc[pl.ds(at, rows), b * length : (b + 1) * length].astype(BF16)


def backward_of(t, ga, query, key, value, probs, key_weight, value_weight, piece):
    rows, cols = query.shape
    tokens, width = key.shape[0], key_weight.shape[0]
    spans = rows // SPAN
    step = 2 * HEAD
    col = lambda n: pl.BlockSpec((n, step), lambda j, t: (0, j))
    return pl.pallas_call(
        functools.partial(backward_kernel, 1.0 / math.sqrt(HEAD)),
        out_shape=[jax.ShapeDtypeStruct((rows, cols), BF16)] + [jax.ShapeDtypeStruct(piece, BF16)] * 4,
        grid_spec=pltpu.PrefetchScalarGridSpec(
            num_scalar_prefetch=1,
            grid=(cols // step,),
            in_specs=[
                col(rows),
                col(rows),
                col(tokens),
                col(tokens),
                pl.BlockSpec((2, spans, SPAN, tokens // spans), lambda j, t: (j, 0, 0, 0)),
                col(width),
                col(width),
            ],
            out_specs=[col(rows)] + [whole(piece)] * 4,
            scratch_shapes=[
                pltpu.VMEM((tokens, step), BF16),
                pltpu.VMEM((tokens, step), BF16),
                pltpu.VMEM((width, tokens), F32),
            ],
        ),
        compiler_params=params(56),
        cost_estimate=cost(4 * tokens * width * cols, 10e6),
        name="backward",
    )(t, ga, query, key, value, probs, key_weight, value_weight)


def hidden_kernel(t_ref, g_ref, w_ref, o0, o1, o2, o3):
    r = pl.program_id(0)
    for i, o in enumerate((o0, o1, o2, o3)):

        @pl.when(r == i)
        def _():
            o[...] = dot(g_ref[...], w_ref[...], NT).astype(BF16)


def hidden_of(t, grad_query, weight):
    rows, cols = grad_query.shape
    width = weight.shape[0] // 4
    return pl.pallas_call(
        hidden_kernel,
        out_shape=[jax.ShapeDtypeStruct((rows, width), BF16)] * 4,
        grid_spec=pltpu.PrefetchScalarGridSpec(
            num_scalar_prefetch=1,
            grid=(4,),
            in_specs=[
                whole((rows, cols)),
                pl.BlockSpec((width, cols), lambda r, t: ((t[0] + r) % 4, 0)),
            ],
            out_specs=[whole((rows, width))] * 4,
        ),
        compiler_params=params(56),
        cost_estimate=cost(2 * rows * 4 * width * cols, 8 * width * cols),
        name="hidden",
    )(t, grad_query, weight)


def pairs_moved(first, second, gaps, sign):
    n = math.prod(lax.axis_size(a) for a in DP)

    def moved(x, by):
        return lax.ppermute(x, DP, [(i, (i + sign * by) % n) for i in range(n)])

    def branch(index):
        return lambda a, b: (moved(a, index // WINDOW + 1), moved(b, index % WINDOW + 1))

    which = (gaps[0] - 1) * WINDOW + gaps[1] - 1
    return lax.switch(which, [branch(i) for i in range(WINDOW * WINDOW)], first, second)


def delivered(states, gaps):
    n = math.prod(lax.axis_size(a) for a in DP)
    pairs = states[:2], states[2:]
    got = [None, None]
    for by in range(1, WINDOW + 1):
        sent = jnp.where(gaps[0] == by, *pairs)
        came = lax.ppermute(sent, DP, [(i, (i - by) % n) for i in range(n)])
        got = [came if g is None else jnp.where(gaps[k] == by, came, g) for k, g in enumerate(got)]
    return jnp.concatenate(got, axis=0)


def gathered_plane(rows):
    n = lax.axis_size("x")
    along = [rows]
    for s in range(1, n):
        along.append(lax.ppermute(rows, "x", [(i, (i + s) % n) for i in range(n)]))
    return lax.all_gather(jnp.stack(along), "z", axis=0)


def shards(
    hidden,
    grad_out,
    query_weight,
    key_weight,
    value_weight,
    out_weight,
    neighbour_states,
    block_owner,
    slot_target,
):
    n_dp = math.prod(lax.axis_size(a) for a in DP)
    t = jnp.stack([lax.axis_index(a) for a in ("tensor", "core", "x")]).astype(jnp.int32)
    plane = gathered_plane(out_weight.T)

    gap = (block_owner[0] - lax.axis_index(DP) + n_dp) % n_dp
    gaps = (gap[0], gap[2])
    hidden_pieces = from_peers(hidden)
    mine = delivered(jnp.swapaxes(neighbour_states, 1, 2), gaps)
    neighbours = from_peers(mine)
    grad_pieces = from_peers(grad_out)

    query = query_of(t, hidden_pieces, query_weight)
    key, value, probs, attended = forward_of(t, query, neighbours, key_weight, value_weight)
    plane = tied(plane, attended)
    other_plane = lax.ppermute(plane, "core", [(0, 1), (1, 0)])
    out_parts, grad_attended = output_of(t, attended, grad_pieces, plane, other_plane)
    cross_out = lax.psum_scatter(
        out_parts.reshape(-1, out_parts.shape[-1]), "tensor", scatter_dimension=0, tiled=True
    )
    grad_query, *state_parts = backward_of(
        t, grad_attended, query, key, value, probs, key_weight, value_weight, mine.shape
    )
    hidden_parts = hidden_of(t, grad_query, query_weight)
    grads = summed(to_peers(state_parts))
    grad_hidden = summed(to_peers(hidden_parts))
    first, second = pairs_moved(grads[:2], grads[2:], gaps, 1)
    grad_states = jnp.swapaxes(jnp.concatenate([first, second], axis=0), 1, 2)
    return cross_out, grad_hidden, grad_states


def solution(mesh):
    grid = Mesh(mesh.devices.reshape(8, 4, 2, 4), DP + ("tensor",))
    placed = (
        P(DP, "tensor"),
        P(DP, "tensor"),
        P(None, "tensor"),
        P(None, "tensor"),
        P(None, "tensor"),
        P("tensor", DP),
        P(DP, None, "tensor"),
        P(DP, None),
        P(DP, None),
    )
    return jax.shard_map(
        shards,
        mesh=grid,
        in_specs=placed,
        out_specs=(P(DP, "tensor"), P(DP, "tensor"), P(DP, None, "tensor")),
        check_vma=False,
    )
```

```python
import functools
import math

import jax
import jax.numpy as jnp
from jax import lax
from jax.experimental import pallas as pl
from jax.experimental.pallas import tpu as pltpu
from jax.sharding import Mesh, PartitionSpec as P

HEAD = 128
SPAN = 64
NBR = 128
WINDOW = 4
DP = ("z", "x", "core")
MIB = 1024 * 1024
F32, BF16 = jnp.float32, jnp.bfloat16

NN = (((1,), (0,)), ((), ()))
NT = (((1,), (1,)), ((), ()))
TN = (((0,), (0,)), ((), ()))


def dot(a, b, dims=NN):
    return lax.dot_general(a, b, dims, preferred_element_type=F32)


def params(mib):
    return pltpu.CompilerParams(vmem_limit_bytes=mib * MIB)


ANY = pl.BlockSpec(memory_space=pl.ANY)
SMEM = pl.BlockSpec(memory_space=pltpu.SMEM)


def whole(shape):
    return pl.BlockSpec(shape, lambda *_: (0,) * len(shape))


def cost(flops, nbytes):
    return pl.CostEstimate(flops=int(flops), bytes_accessed=int(nbytes), transcendentals=0)


def from_peers(x):
    n = lax.axis_size("tensor")
    got = [x]
    for r in range(1, n):
        got.append(lax.ppermute(x, "tensor", [((i + r) % n, i) for i in range(n)]))
    return got


def to_peers(pieces):
    n = lax.axis_size("tensor")
    got = [pieces[0]]
    for r in range(1, n):
        got.append(lax.ppermute(pieces[r], "tensor", [(i, (i + r) % n) for i in range(n)]))
    return got


def exchanged(x):
    return lax.all_to_all(x, "tensor", split_axis=0, concat_axis=0, tiled=True)


def summed(parts):
    total = parts[0].astype(F32)
    for part in parts[1:]:
        total = total + part.astype(F32)
    return total.astype(BF16)


def nothing(*_):
    pass


def tied(x, *after):
    return pl.pallas_call(
        nothing,
        out_shape=jax.ShapeDtypeStruct(x.shape, x.dtype),
        in_specs=[ANY] * (1 + len(after)),
        out_specs=ANY,
        input_output_aliases={0: 0},
        name="tied",
    )(x, *after)


def query_kernel(h_ref, w_ref, q_ref, acc):
    i, last = pl.program_id(0), pl.num_programs(0) - 1
    part = dot(h_ref[0], w_ref[...])

    @pl.when(i == 0)
    def _():
        acc[...] = part

    @pl.when(jnp.logical_and(i > 0, i < last))
    def _():
        acc[...] += part

    @pl.when(i == last)
    def _():
        q_ref[...] = (acc[...] + part).astype(BF16)


def query_of(pieces, weight):
    steps, rows, width = pieces.shape
    rows, cols = rows // 2, weight.shape[1]
    return pl.pallas_call(
        query_kernel,
        out_shape=jax.ShapeDtypeStruct((rows, cols), BF16),
        grid=(steps,),
        in_specs=[
            pl.BlockSpec((1, rows, width), lambda i: (i, 0, 0)),
            pl.BlockSpec((width, cols), lambda i: (i, 0)),
        ],
        out_specs=whole((rows, cols)),
        scratch_shapes=[pltpu.VMEM((rows, cols), F32)],
        compiler_params=params(56),
        cost_estimate=cost(2 * rows * steps * width * cols, 2 * steps * width * cols),
        name="query",
    )(pieces, weight)


def forward_kernel(
    scale, t_ref, q_ref, n0, n1, n2, n3, kw_ref, vw_ref, k_ref, v_ref, p_ref, a_ref, flipped, rows
):
    blocks, part, length = n0.shape

    @pl.when(pl.program_id(0) == 0)
    def _():
        for r, n in enumerate((n0, n1, n2, n3)):
            at = pl.multiple_of(((t_ref[0] + r) % 4) * part, part)
            for b in range(blocks):
                flipped[pl.ds(at, part), b * length : (b + 1) * length] = n[b]
        rows[...] = flipped[...].T

    k_ref[...] = dot(rows[...], kw_ref[...]).astype(BF16)
    v_ref[...] = dot(rows[...], vw_ref[...]).astype(BF16)
    spans = q_ref.shape[0] // SPAN
    keys = k_ref.shape[0] // spans
    for j in range(q_ref.shape[1] // HEAD):
        c = slice(j * HEAD, (j + 1) * HEAD)
        for s in range(spans):
            qs = slice(s * SPAN, (s + 1) * SPAN)
            ks = slice(s * keys, (s + 1) * keys)
            scores = dot(q_ref[qs, c], k_ref[ks, c], NT) * scale
            e = jnp.exp(scores - jnp.max(scores, axis=-1, keepdims=True))
            probs = e / jnp.sum(e, axis=-1, keepdims=True)
            p_ref[j, s] = probs
            a_ref[qs, c] = dot(probs.astype(BF16), v_ref[ks, c]).astype(BF16)


def forward_of(t, query, pieces, key_weight, value_weight):
    rows, cols = query.shape
    blocks, part, length = pieces[0].shape
    tokens, width = blocks * length, key_weight.shape[0]
    spans = rows // SPAN
    step = 2 * HEAD
    col = lambda n: pl.BlockSpec((n, step), lambda j, t: (0, j))
    return pl.pallas_call(
        functools.partial(forward_kernel, 1.0 / math.sqrt(HEAD)),
        out_shape=(
            jax.ShapeDtypeStruct((tokens, cols), BF16),
            jax.ShapeDtypeStruct((tokens, cols), BF16),
            jax.ShapeDtypeStruct((cols // HEAD, spans, SPAN, tokens // spans), F32),
            jax.ShapeDtypeStruct((rows, cols), BF16),
        ),
        grid_spec=pltpu.PrefetchScalarGridSpec(
            num_scalar_prefetch=1,
            grid=(cols // step,),
            in_specs=[col(rows)] + [whole(pieces[0].shape)] * 4 + [col(width)] * 2,
            out_specs=[
                col(tokens),
                col(tokens),
                pl.BlockSpec((2, spans, SPAN, tokens // spans), lambda j, t: (j, 0, 0, 0)),
                col(rows),
            ],
            scratch_shapes=[pltpu.VMEM((width, tokens), BF16), pltpu.VMEM((tokens, width), BF16)],
        ),
        compiler_params=params(56),
        cost_estimate=cost(4 * tokens * width * cols, 10e6),
        name="forward",
    )(t, query, *pieces, key_weight, value_weight)


def output_kernel(t_ref, a_ref, g_ref, own, other, o_ref, ga_ref, w_ref, sems):
    core, x = t_ref[1], t_ref[2]
    steps, _, width = g_ref.shape
    chips = own.shape[1]
    deep = own.shape[0] // steps
    copies = []
    for i in range(steps):
        for s in range(chips):
            at = (x - s + chips) % chips
            for n, (plane, c) in enumerate(((own, core), (other, 1 - core))):
                copies.append(
                    pltpu.make_async_copy(
                        plane.at[pl.ds(i * deep, deep), s], w_ref.at[i, :, at, c], sems.at[i, 2 * s + n]
                    )
                )
    for copy in copies:
        copy.start()
    total = None
    for i in range(steps):
        for copy in copies[i * 2 * chips : (i + 1) * 2 * chips]:
            copy.wait()
        w = w_ref[i].reshape(width, a_ref.shape[1])
        part = dot(g_ref[i], w)
        total = part if total is None else total + part
        o_ref[i] = dot(a_ref[...], w, NT).astype(BF16)
    ga_ref[...] = total.astype(BF16)


def output_of(t, attended, pieces, own, other):
    rows, cols = attended.shape
    steps, _, width = pieces.shape
    deep, chips = own.shape[0] // steps, own.shape[1]
    return pl.pallas_call(
        output_kernel,
        out_shape=(
            jax.ShapeDtypeStruct((steps, rows, width), BF16),
            jax.ShapeDtypeStruct((rows, cols), BF16),
        ),
        grid=(1,),
        in_specs=[
            SMEM,
            whole((rows, cols)),
            pl.BlockSpec((steps, rows, width), lambda i: (0, 1, 0)),
            ANY,
            ANY,
        ],
        out_specs=(whole((steps, rows, width)), whole((rows, cols))),
        scratch_shapes=[
            pltpu.VMEM((steps, deep, chips, 2, *own.shape[2:]), BF16),
            pltpu.SemaphoreType.DMA((steps, 2 * chips)),
        ],
        compiler_params=params(28),
        cost_estimate=cost(4 * rows * steps * width * cols, 2 * steps * width * cols),
        name="output",
    )(t, attended, pieces, own, other)


def backward_kernel(
    scale, t_ref, ga_ref, q_ref, k_ref, v_ref, p_ref, kw_ref, vw_ref, gq_ref, s0, s1, s2, s3, gk, gv, acc
):
    j, last = pl.program_id(0), pl.num_programs(0) - 1
    spans = q_ref.shape[0] // SPAN
    keys = k_ref.shape[0] // spans
    for h in range(q_ref.shape[1] // HEAD):
        c = slice(h * HEAD, (h + 1) * HEAD)
        for s in range(spans):
            qs = slice(s * SPAN, (s + 1) * SPAN)
            ks = slice(s * keys, (s + 1) * keys)
            probs, ga = p_ref[h, s], ga_ref[qs, c]
            gp = dot(ga, v_ref[ks, c], NT)
            inner = jnp.sum(probs * gp, axis=-1, keepdims=True)
            gs = (probs * (gp - inner) * scale).astype(BF16)
            gq_ref[qs, c] = dot(gs, k_ref[ks, c]).astype(BF16)
            gk[ks, c] = dot(gs, q_ref[qs, c], TN).astype(BF16)
            gv[ks, c] = dot(probs.astype(BF16), ga, TN).astype(BF16)
    part = dot(kw_ref[...], gk[...], NT) + dot(vw_ref[...], gv[...], NT)

    @pl.when(j == 0)
    def _():
        acc[...] = part

    @pl.when(j > 0)
    def _():
        acc[...] += part

    @pl.when(j == last)
    def _():
        blocks, rows, length = s0.shape
        for r, out in enumerate((s0, s1, s2, s3)):
            at = pl.multiple_of(((t_ref[0] + r) % 4) * rows, rows)
            for b in range(blocks):
                out[b] = acc[pl.ds(at, rows), b * length : (b + 1) * length].astype(BF16)


def backward_of(t, ga, query, key, value, probs, key_weight, value_weight, piece):
    rows, cols = query.shape
    tokens, width = key.shape[0], key_weight.shape[0]
    spans = rows // SPAN
    step = 2 * HEAD
    col = lambda n: pl.BlockSpec((n, step), lambda j, t: (0, j))
    return pl.pallas_call(
        functools.partial(backward_kernel, 1.0 / math.sqrt(HEAD)),
        out_shape=[jax.ShapeDtypeStruct((rows, cols), BF16)] + [jax.ShapeDtypeStruct(piece, BF16)] * 4,
        grid_spec=pltpu.PrefetchScalarGridSpec(
            num_scalar_prefetch=1,
            grid=(cols // step,),
            in_specs=[
                col(rows),
                col(rows),
                col(tokens),
                col(tokens),
                pl.BlockSpec((2, spans, SPAN, tokens // spans), lambda j, t: (j, 0, 0, 0)),
                col(width),
                col(width),
            ],
            out_specs=[col(rows)] + [whole(piece)] * 4,
            scratch_shapes=[
                pltpu.VMEM((tokens, step), BF16),
                pltpu.VMEM((tokens, step), BF16),
                pltpu.VMEM((width, tokens), F32),
            ],
        ),
        compiler_params=params(56),
        cost_estimate=cost(4 * tokens * width * cols, 10e6),
        name="backward",
    )(t, ga, query, key, value, probs, key_weight, value_weight)


def hidden_kernel(g_ref, w_ref, o_ref):
    o_ref[0] = dot(g_ref[...], w_ref[...], NT).astype(BF16)


def hidden_of(grad_query, weight):
    rows, cols = grad_query.shape
    width = weight.shape[0] // 4
    return pl.pallas_call(
        hidden_kernel,
        out_shape=jax.ShapeDtypeStruct((4, rows, width), BF16),
        grid=(4,),
        in_specs=[whole((rows, cols)), pl.BlockSpec((width, cols), lambda i: (i, 0))],
        out_specs=pl.BlockSpec((1, rows, width), lambda i: (i, 0, 0)),
        compiler_params=params(56),
        cost_estimate=cost(2 * rows * 4 * width * cols, 8 * width * cols),
        name="hidden",
    )(grad_query, weight)


def pairs_moved(first, second, gaps, sign):
    n = math.prod(lax.axis_size(a) for a in DP)

    def moved(x, by):
        return lax.ppermute(x, DP, [(i, (i + sign * by) % n) for i in range(n)])

    def branch(index):
        return lambda a, b: (moved(a, index // WINDOW + 1), moved(b, index % WINDOW + 1))

    which = (gaps[0] - 1) * WINDOW + gaps[1] - 1
    return lax.switch(which, [branch(i) for i in range(WINDOW * WINDOW)], first, second)


def delivered(states, gaps):
    n = math.prod(lax.axis_size(a) for a in DP)
    pairs = states[:2], states[2:]
    got = [None, None]
    for by in range(1, WINDOW + 1):
        sent = jnp.where(gaps[0] == by, *pairs)
        came = lax.ppermute(sent, DP, [(i, (i - by) % n) for i in range(n)])
        got = [came if g is None else jnp.where(gaps[k] == by, came, g) for k, g in enumerate(got)]
    return jnp.concatenate(got, axis=0)


def gathered_plane(rows):
    n = lax.axis_size("x")
    along = [rows]
    for s in range(1, n):
        along.append(lax.ppermute(rows, "x", [(i, (i + s) % n) for i in range(n)]))
    return lax.all_gather(jnp.stack(along), "z", axis=0)


def shards(
    hidden,
    grad_out,
    query_weight,
    key_weight,
    value_weight,
    out_weight,
    neighbour_states,
    block_owner,
    slot_target,
):
    n_dp = math.prod(lax.axis_size(a) for a in DP)
    t = jnp.stack([lax.axis_index(a) for a in ("tensor", "core", "x")]).astype(jnp.int32)
    plane = gathered_plane(out_weight.T)

    gap = (block_owner[0] - lax.axis_index(DP) + n_dp) % n_dp
    gaps = (gap[0], gap[2])
    both = jnp.concatenate([hidden, grad_out], axis=0)
    pieces = exchanged(jnp.broadcast_to(both, (lax.axis_size("tensor"), *both.shape)))
    pieces = pieces.reshape(-1, *both.shape)
    mine = delivered(jnp.swapaxes(neighbour_states, 1, 2), gaps)
    neighbours = from_peers(mine)

    query = query_of(pieces, query_weight)
    key, value, probs, attended = forward_of(t, query, neighbours, key_weight, value_weight)
    plane = tied(plane, attended)
    other_plane = lax.ppermute(plane, "core", [(0, 1), (1, 0)])
    out_parts, grad_attended = output_of(t, attended, pieces, plane, other_plane)
    cross_out = summed(exchanged(out_parts))
    grad_query, *state_parts = backward_of(
        t, grad_attended, query, key, value, probs, key_weight, value_weight, mine.shape
    )
    grad_hidden = summed(exchanged(hidden_of(grad_query, query_weight)))
    grads = summed(to_peers(state_parts))
    first, second = pairs_moved(grads[:2], grads[2:], gaps, 1)
    grad_states = jnp.swapaxes(jnp.concatenate([first, second], axis=0), 1, 2)
    return cross_out, grad_hidden, grad_states


def solution(mesh):
    grid = Mesh(mesh.devices.reshape(8, 4, 2, 4), DP + ("tensor",))
    placed = (
        P(DP, "tensor"),
        P(DP, "tensor"),
        P(None, "tensor"),
        P(None, "tensor"),
        P(None, "tensor"),
        P("tensor", DP),
        P(DP, None, "tensor"),
        P(DP, None),
        P(DP, None),
    )
    return jax.shard_map(
        shards,
        mesh=grid,
        in_specs=placed,
        out_specs=(P(DP, "tensor"), P(DP, "tensor"), P(DP, None, "tensor")),
        check_vma=False,
    )
```

```python
import functools
import math

import jax
import jax.numpy as jnp
from jax import lax
from jax.experimental import pallas as pl
from jax.experimental.pallas import tpu as pltpu
from jax.sharding import Mesh, PartitionSpec as P

HEAD = 128
SPAN = 64
NBR = 128
WINDOW = 4
DP = ("z", "x", "core")
MIB = 1024 * 1024
F32, BF16 = jnp.float32, jnp.bfloat16

NN = (((1,), (0,)), ((), ()))
NT = (((1,), (1,)), ((), ()))
TN = (((0,), (0,)), ((), ()))


def dot(a, b, dims=NN):
    return lax.dot_general(a, b, dims, preferred_element_type=F32)


def params(mib):
    return pltpu.CompilerParams(vmem_limit_bytes=mib * MIB)


ANY = pl.BlockSpec(memory_space=pl.ANY)
SMEM = pl.BlockSpec(memory_space=pltpu.SMEM)


def whole(shape):
    return pl.BlockSpec(shape, lambda *_: (0,) * len(shape))


def cost(flops, nbytes):
    return pl.CostEstimate(flops=int(flops), bytes_accessed=int(nbytes), transcendentals=0)


def from_peers(x):
    n = lax.axis_size("tensor")
    got = [x]
    for r in range(1, n):
        got.append(lax.ppermute(x, "tensor", [((i + r) % n, i) for i in range(n)]))
    return got


def to_peers(pieces):
    n = lax.axis_size("tensor")
    got = [pieces[0]]
    for r in range(1, n):
        got.append(lax.ppermute(pieces[r], "tensor", [(i, (i + r) % n) for i in range(n)]))
    return got


def exchanged(x):
    return lax.all_to_all(x, "tensor", split_axis=0, concat_axis=0, tiled=True)


def summed(parts):
    total = parts[0].astype(F32)
    for part in parts[1:]:
        total = total + part.astype(F32)
    return total.astype(BF16)


def nothing(*_):
    pass


def tied(x, *after):
    return pl.pallas_call(
        nothing,
        out_shape=jax.ShapeDtypeStruct(x.shape, x.dtype),
        in_specs=[ANY] * (1 + len(after)),
        out_specs=ANY,
        input_output_aliases={0: 0},
        name="tied",
    )(x, *after)


def query_kernel(h_ref, w_ref, q_ref, acc):
    i, last = pl.program_id(0), pl.num_programs(0) - 1
    part = dot(h_ref[0], w_ref[...])

    @pl.when(i == 0)
    def _():
        acc[...] = part

    @pl.when(jnp.logical_and(i > 0, i < last))
    def _():
        acc[...] += part

    @pl.when(i == last)
    def _():
        q_ref[...] = (acc[...] + part).astype(BF16)


def query_of(pieces, weight):
    steps, rows, width = pieces.shape
    rows, cols = rows // 2, weight.shape[1]
    return pl.pallas_call(
        query_kernel,
        out_shape=jax.ShapeDtypeStruct((rows, cols), BF16),
        grid=(steps,),
        in_specs=[
            pl.BlockSpec((1, rows, width), lambda i: (i, 0, 0)),
            pl.BlockSpec((width, cols), lambda i: (i, 0)),
        ],
        out_specs=whole((rows, cols)),
        scratch_shapes=[pltpu.VMEM((rows, cols), F32)],
        compiler_params=params(56),
        cost_estimate=cost(2 * rows * steps * width * cols, 2 * steps * width * cols),
        name="query",
    )(pieces, weight)


def forward_kernel(
    scale, t_ref, q_ref, n0, n1, n2, n3, kw_ref, vw_ref, k_ref, v_ref, p_ref, a_ref, flipped, rows
):
    blocks, part, length = n0.shape

    @pl.when(pl.program_id(0) == 0)
    def _():
        for r, n in enumerate((n0, n1, n2, n3)):
            at = pl.multiple_of(((t_ref[0] + r) % 4) * part, part)
            for b in range(blocks):
                flipped[pl.ds(at, part), b * length : (b + 1) * length] = n[b]
        rows[...] = flipped[...].T

    k_ref[...] = dot(rows[...], kw_ref[...]).astype(BF16)
    v_ref[...] = dot(rows[...], vw_ref[...]).astype(BF16)
    spans = q_ref.shape[0] // SPAN
    keys = k_ref.shape[0] // spans
    for j in range(q_ref.shape[1] // HEAD):
        c = slice(j * HEAD, (j + 1) * HEAD)
        for s in range(spans):
            qs = slice(s * SPAN, (s + 1) * SPAN)
            ks = slice(s * keys, (s + 1) * keys)
            scores = dot(q_ref[qs, c], k_ref[ks, c], NT) * scale
            e = jnp.exp(scores - jnp.max(scores, axis=-1, keepdims=True))
            probs = e / jnp.sum(e, axis=-1, keepdims=True)
            p_ref[j, s] = probs
            a_ref[qs, c] = dot(probs.astype(BF16), v_ref[ks, c]).astype(BF16)


def forward_of(t, query, pieces, key_weight, value_weight):
    rows, cols = query.shape
    blocks, part, length = pieces[0].shape
    tokens, width = blocks * length, key_weight.shape[0]
    spans = rows // SPAN
    step = 2 * HEAD
    col = lambda n: pl.BlockSpec((n, step), lambda j, t: (0, j))
    return pl.pallas_call(
        functools.partial(forward_kernel, 1.0 / math.sqrt(HEAD)),
        out_shape=(
            jax.ShapeDtypeStruct((tokens, cols), BF16),
            jax.ShapeDtypeStruct((tokens, cols), BF16),
            jax.ShapeDtypeStruct((cols // HEAD, spans, SPAN, tokens // spans), F32),
            jax.ShapeDtypeStruct((rows, cols), BF16),
        ),
        grid_spec=pltpu.PrefetchScalarGridSpec(
            num_scalar_prefetch=1,
            grid=(cols // step,),
            in_specs=[col(rows)] + [whole(pieces[0].shape)] * 4 + [col(width)] * 2,
            out_specs=[
                col(tokens),
                col(tokens),
                pl.BlockSpec((2, spans, SPAN, tokens // spans), lambda j, t: (j, 0, 0, 0)),
                col(rows),
            ],
            scratch_shapes=[pltpu.VMEM((width, tokens), BF16), pltpu.VMEM((tokens, width), BF16)],
        ),
        compiler_params=params(56),
        cost_estimate=cost(4 * tokens * width * cols, 10e6),
        name="forward",
    )(t, query, *pieces, key_weight, value_weight)


def output_kernel(t_ref, a_ref, g_ref, own, other, o_ref, ga_ref, w_ref, sems):
    core, x = t_ref[1], t_ref[2]
    steps, _, width = g_ref.shape
    chips = own.shape[1]
    deep = own.shape[0] // steps
    copies = []
    for i in range(steps):
        for s in range(chips):
            at = (x - s + chips) % chips
            for n, (plane, c) in enumerate(((own, core), (other, 1 - core))):
                copies.append(
                    pltpu.make_async_copy(
                        plane.at[pl.ds(i * deep, deep), s], w_ref.at[i, :, at, c], sems.at[i, 2 * s + n]
                    )
                )
    for copy in copies:
        copy.start()
    total = None
    for i in range(steps):
        for copy in copies[i * 2 * chips : (i + 1) * 2 * chips]:
            copy.wait()
        w = w_ref[i].reshape(width, a_ref.shape[1])
        part = dot(g_ref[i], w)
        total = part if total is None else total + part
        o_ref[i] = dot(a_ref[...], w, NT).astype(BF16)
    ga_ref[...] = total.astype(BF16)


def output_of(t, attended, pieces, own, other):
    rows, cols = attended.shape
    steps, _, width = pieces.shape
    deep, chips = own.shape[0] // steps, own.shape[1]
    return pl.pallas_call(
        output_kernel,
        out_shape=(
            jax.ShapeDtypeStruct((steps, rows, width), BF16),
            jax.ShapeDtypeStruct((rows, cols), BF16),
        ),
        grid=(1,),
        in_specs=[
            SMEM,
            whole((rows, cols)),
            pl.BlockSpec((steps, rows, width), lambda i: (0, 1, 0)),
            ANY,
            ANY,
        ],
        out_specs=(whole((steps, rows, width)), whole((rows, cols))),
        scratch_shapes=[
            pltpu.VMEM((steps, deep, chips, 2, *own.shape[2:]), BF16),
            pltpu.SemaphoreType.DMA((steps, 2 * chips)),
        ],
        compiler_params=params(28),
        cost_estimate=cost(4 * rows * steps * width * cols, 2 * steps * width * cols),
        name="output",
    )(t, attended, pieces, own, other)


def backward_kernel(
    scale, t_ref, ga_ref, q_ref, k_ref, v_ref, p_ref, kw_ref, vw_ref, gq_ref, s0, s1, s2, s3, gk, gv, acc
):
    j, last = pl.program_id(0), pl.num_programs(0) - 1
    spans = q_ref.shape[0] // SPAN
    keys = k_ref.shape[0] // spans
    for h in range(q_ref.shape[1] // HEAD):
        c = slice(h * HEAD, (h + 1) * HEAD)
        for s in range(spans):
            qs = slice(s * SPAN, (s + 1) * SPAN)
            ks = slice(s * keys, (s + 1) * keys)
            probs, ga = p_ref[h, s], ga_ref[qs, c]
            gp = dot(ga, v_ref[ks, c], NT)
            inner = jnp.sum(probs * gp, axis=-1, keepdims=True)
            gs = (probs * (gp - inner) * scale).astype(BF16)
            gq_ref[qs, c] = dot(gs, k_ref[ks, c]).astype(BF16)
            gk[ks, c] = dot(gs, q_ref[qs, c], TN).astype(BF16)
            gv[ks, c] = dot(probs.astype(BF16), ga, TN).astype(BF16)
    part = dot(kw_ref[...], gk[...], NT) + dot(vw_ref[...], gv[...], NT)

    @pl.when(j == 0)
    def _():
        acc[...] = part

    @pl.when(j > 0)
    def _():
        acc[...] += part

    @pl.when(j == last)
    def _():
        blocks, rows, length = s0.shape
        for r, out in enumerate((s0, s1, s2, s3)):
            at = pl.multiple_of(((t_ref[0] + r) % 4) * rows, rows)
            for b in range(blocks):
                out[b] = acc[pl.ds(at, rows), b * length : (b + 1) * length].astype(BF16)


def backward_of(t, ga, query, key, value, probs, key_weight, value_weight, piece):
    rows, cols = query.shape
    tokens, width = key.shape[0], key_weight.shape[0]
    spans = rows // SPAN
    step = 2 * HEAD
    col = lambda n: pl.BlockSpec((n, step), lambda j, t: (0, j))
    return pl.pallas_call(
        functools.partial(backward_kernel, 1.0 / math.sqrt(HEAD)),
        out_shape=[jax.ShapeDtypeStruct((rows, cols), BF16)] + [jax.ShapeDtypeStruct(piece, BF16)] * 4,
        grid_spec=pltpu.PrefetchScalarGridSpec(
            num_scalar_prefetch=1,
            grid=(cols // step,),
            in_specs=[
                col(rows),
                col(rows),
                col(tokens),
                col(tokens),
                pl.BlockSpec((2, spans, SPAN, tokens // spans), lambda j, t: (j, 0, 0, 0)),
                col(width),
                col(width),
            ],
            out_specs=[col(rows)] + [whole(piece)] * 4,
            scratch_shapes=[
                pltpu.VMEM((tokens, step), BF16),
                pltpu.VMEM((tokens, step), BF16),
                pltpu.VMEM((width, tokens), F32),
            ],
        ),
        compiler_params=params(56),
        cost_estimate=cost(4 * tokens * width * cols, 10e6),
        name="backward",
    )(t, ga, query, key, value, probs, key_weight, value_weight)


def hidden_kernel(g_ref, w_ref, o_ref):
    o_ref[0] = dot(g_ref[...], w_ref[...], NT).astype(BF16)


def hidden_of(grad_query, weight):
    rows, cols = grad_query.shape
    width = weight.shape[0] // 4
    return pl.pallas_call(
        hidden_kernel,
        out_shape=jax.ShapeDtypeStruct((4, rows, width), BF16),
        grid=(4,),
        in_specs=[whole((rows, cols)), pl.BlockSpec((width, cols), lambda i: (i, 0))],
        out_specs=pl.BlockSpec((1, rows, width), lambda i: (i, 0, 0)),
        compiler_params=params(56),
        cost_estimate=cost(2 * rows * 4 * width * cols, 8 * width * cols),
        name="hidden",
    )(grad_query, weight)


def pairs_moved(blocks, gaps, sign):
    n = math.prod(lax.axis_size(a) for a in DP)
    pairs = blocks[:2], blocks[2:]
    got = [None, None]
    for by in range(1, WINDOW + 1):
        sent = jnp.where(gaps[0] == by, *pairs)
        came = lax.ppermute(sent, DP, [(i, (i + sign * by) % n) for i in range(n)])
        got = [came if g is None else jnp.where(gaps[k] == by, came, g) for k, g in enumerate(got)]
    return jnp.concatenate(got, axis=0)


def gathered_plane(rows):
    n = lax.axis_size("x")
    along = [rows]
    for s in range(1, n):
        along.append(lax.ppermute(rows, "x", [(i, (i + s) % n) for i in range(n)]))
    return lax.all_gather(jnp.stack(along), "z", axis=0)


def shards(
    hidden,
    grad_out,
    query_weight,
    key_weight,
    value_weight,
    out_weight,
    neighbour_states,
    block_owner,
    slot_target,
):
    n_dp = math.prod(lax.axis_size(a) for a in DP)
    t = jnp.stack([lax.axis_index(a) for a in ("tensor", "core", "x")]).astype(jnp.int32)
    plane = gathered_plane(out_weight.T)

    gap = (block_owner[0] - lax.axis_index(DP) + n_dp) % n_dp
    gaps = (gap[0], gap[2])
    both = jnp.concatenate([hidden, grad_out], axis=0)
    pieces = exchanged(jnp.broadcast_to(both, (lax.axis_size("tensor"), *both.shape)))
    pieces = pieces.reshape(-1, *both.shape)
    mine = pairs_moved(jnp.swapaxes(neighbour_states, 1, 2), gaps, -1)
    neighbours = from_peers(mine)

    query = query_of(pieces, query_weight)
    key, value, probs, attended = forward_of(t, query, neighbours, key_weight, value_weight)
    plane = tied(plane, attended)
    other_plane = lax.ppermute(plane, "core", [(0, 1), (1, 0)])
    out_parts, grad_attended = output_of(t, attended, pieces, plane, other_plane)
    cross_out = summed(exchanged(out_parts))
    grad_query, *state_parts = backward_of(
        t, grad_attended, query, key, value, probs, key_weight, value_weight, mine.shape
    )
    grad_hidden = summed(exchanged(hidden_of(grad_query, query_weight)))
    grads = summed(to_peers(state_parts))
    grad_states = jnp.swapaxes(pairs_moved(grads, gaps, 1), 1, 2)
    return cross_out, grad_hidden, grad_states


def solution(mesh):
    grid = Mesh(mesh.devices.reshape(8, 4, 2, 4), DP + ("tensor",))
    placed = (
        P(DP, "tensor"),
        P(DP, "tensor"),
        P(None, "tensor"),
        P(None, "tensor"),
        P(None, "tensor"),
        P("tensor", DP),
        P(DP, None, "tensor"),
        P(DP, None),
        P(DP, None),
    )
    return jax.shard_map(
        shards,
        mesh=grid,
        in_specs=placed,
        out_specs=(P(DP, "tensor"), P(DP, "tensor"), P(DP, None, "tensor")),
        check_vma=False,
    )
```

```python
import functools
import math

import jax
import jax.numpy as jnp
from jax import lax
from jax.experimental import pallas as pl
from jax.experimental.pallas import tpu as pltpu
from jax.sharding import Mesh, PartitionSpec as P

HEAD = 128
SPAN = 64
NBR = 128
WINDOW = 4
DP = ("z", "x", "core")
MIB = 1024 * 1024
F32, BF16 = jnp.float32, jnp.bfloat16

NN = (((1,), (0,)), ((), ()))
NT = (((1,), (1,)), ((), ()))
TN = (((0,), (0,)), ((), ()))


def dot(a, b, dims=NN):
    return lax.dot_general(a, b, dims, preferred_element_type=F32)


def params(mib):
    return pltpu.CompilerParams(vmem_limit_bytes=mib * MIB)


ANY = pl.BlockSpec(memory_space=pl.ANY)
SMEM = pl.BlockSpec(memory_space=pltpu.SMEM)


def whole(shape):
    return pl.BlockSpec(shape, lambda *_: (0,) * len(shape))


def cost(flops, nbytes):
    return pl.CostEstimate(flops=int(flops), bytes_accessed=int(nbytes), transcendentals=0)


def from_peers(x):
    n = lax.axis_size("tensor")
    got = [x]
    for r in range(1, n):
        got.append(lax.ppermute(x, "tensor", [((i + r) % n, i) for i in range(n)]))
    return got


def to_peers(pieces):
    n = lax.axis_size("tensor")
    got = [pieces[0]]
    for r in range(1, n):
        got.append(lax.ppermute(pieces[r], "tensor", [(i, (i + r) % n) for i in range(n)]))
    return got


def exchanged(x):
    return lax.all_to_all(x, "tensor", split_axis=0, concat_axis=0, tiled=True)


def summed(parts):
    total = parts[0].astype(F32)
    for part in parts[1:]:
        total = total + part.astype(F32)
    return total.astype(BF16)


def nothing(*_):
    pass


def tied(x, *after):
    return pl.pallas_call(
        nothing,
        out_shape=jax.ShapeDtypeStruct(x.shape, x.dtype),
        in_specs=[ANY] * (1 + len(after)),
        out_specs=ANY,
        input_output_aliases={0: 0},
        name="tied",
    )(x, *after)


def query_kernel(h_ref, w_ref, q_ref, acc):
    i, last = pl.program_id(0), pl.num_programs(0) - 1
    part = dot(h_ref[0], w_ref[...])

    @pl.when(i == 0)
    def _():
        acc[...] = part

    @pl.when(jnp.logical_and(i > 0, i < last))
    def _():
        acc[...] += part

    @pl.when(i == last)
    def _():
        q_ref[...] = (acc[...] + part).astype(BF16)


def query_of(pieces, weight):
    steps, rows, width = pieces.shape
    rows, cols = rows // 2, weight.shape[1]
    return pl.pallas_call(
        query_kernel,
        out_shape=jax.ShapeDtypeStruct((rows, cols), BF16),
        grid=(steps,),
        in_specs=[
            pl.BlockSpec((1, rows, width), lambda i: (i, 0, 0)),
            pl.BlockSpec((width, cols), lambda i: (i, 0)),
        ],
        out_specs=whole((rows, cols)),
        scratch_shapes=[pltpu.VMEM((rows, cols), F32)],
        compiler_params=params(56),
        cost_estimate=cost(2 * rows * steps * width * cols, 2 * steps * width * cols),
        name="query",
    )(pieces, weight)


def forward_kernel(
    scale, t_ref, q_ref, n0, n1, n2, n3, kw_ref, vw_ref, k_ref, v_ref, p_ref, a_ref, flipped, rows
):
    blocks, part, length = n0.shape

    @pl.when(pl.program_id(0) == 0)
    def _():
        for r, n in enumerate((n0, n1, n2, n3)):
            at = pl.multiple_of(((t_ref[0] + r) % 4) * part, part)
            for b in range(blocks):
                flipped[pl.ds(at, part), b * length : (b + 1) * length] = n[b]
        rows[...] = flipped[...].T

    k_ref[...] = dot(rows[...], kw_ref[...]).astype(BF16)
    v_ref[...] = dot(rows[...], vw_ref[...]).astype(BF16)
    spans = q_ref.shape[0] // SPAN
    keys = k_ref.shape[0] // spans
    for j in range(q_ref.shape[1] // HEAD):
        c = slice(j * HEAD, (j + 1) * HEAD)
        for s in range(spans):
            qs = slice(s * SPAN, (s + 1) * SPAN)
            ks = slice(s * keys, (s + 1) * keys)
            scores = dot(q_ref[qs, c], k_ref[ks, c], NT) * scale
            e = jnp.exp(scores - jnp.max(scores, axis=-1, keepdims=True))
            probs = e / jnp.sum(e, axis=-1, keepdims=True)
            p_ref[j, s] = probs
            a_ref[qs, c] = dot(probs.astype(BF16), v_ref[ks, c]).astype(BF16)


def forward_of(t, query, pieces, key_weight, value_weight):
    rows, cols = query.shape
    blocks, part, length = pieces[0].shape
    tokens, width = blocks * length, key_weight.shape[0]
    spans = rows // SPAN
    step = 2 * HEAD
    col = lambda n: pl.BlockSpec((n, step), lambda j, t: (0, j))
    return pl.pallas_call(
        functools.partial(forward_kernel, 1.0 / math.sqrt(HEAD)),
        out_shape=(
            jax.ShapeDtypeStruct((tokens, cols), BF16),
            jax.ShapeDtypeStruct((tokens, cols), BF16),
            jax.ShapeDtypeStruct((cols // HEAD, spans, SPAN, tokens // spans), F32),
            jax.ShapeDtypeStruct((rows, cols), BF16),
        ),
        grid_spec=pltpu.PrefetchScalarGridSpec(
            num_scalar_prefetch=1,
            grid=(cols // step,),
            in_specs=[col(rows)] + [whole(pieces[0].shape)] * 4 + [col(width)] * 2,
            out_specs=[
                col(tokens),
                col(tokens),
                pl.BlockSpec((2, spans, SPAN, tokens // spans), lambda j, t: (j, 0, 0, 0)),
                col(rows),
            ],
            scratch_shapes=[pltpu.VMEM((width, tokens), BF16), pltpu.VMEM((tokens, width), BF16)],
        ),
        compiler_params=params(56),
        cost_estimate=cost(4 * tokens * width * cols, 10e6),
        name="forward",
    )(t, query, *pieces, key_weight, value_weight)


def output_kernel(steps, first, t_ref, a_ref, g_ref, *refs):
    pieces = sum(len(firsts) for _, firsts in steps)
    own, other, refs = refs[:pieces], refs[pieces : 2 * pieces], refs[2 * pieces :]
    if not first:
        o_before, ga_before, *refs = refs
    o_ref, ga_ref, w_ref, sems = refs
    core, x, z = t_ref[1], t_ref[2], t_ref[3]
    chips, deep = w_ref.shape[1], 2 * g_ref.shape[0]
    width = g_ref.shape[2] // 2
    groups = []
    n = 0
    for i, (_, firsts) in enumerate(steps):
        copies = []
        for start in firsts:
            for s in range(own[n].shape[0]):
                at = (x - start - s + chips) % chips
                for plane, c in ((own[n], core), (other[n], 1 - core)):
                    copies.append(
                        pltpu.make_async_copy(plane.at[s], w_ref.at[i, at, c], sems.at[i, len(copies)])
                    )
            n += 1
        groups.append(copies)
    for copies in groups:
        for copy in copies:
            copy.start()
    total = None if first else ga_before[...]
    if not first:
        o_ref[...] = o_before[...]
    for i, (step, _) in enumerate(steps):
        for copy in groups[i]:
            copy.wait()
        w = w_ref[i].reshape(width, a_ref.shape[1])
        row = (z + step + deep) % deep
        cols = pl.ds(pl.multiple_of((row % 2) * width, width), width)
        part = dot(g_ref[row // 2, :, cols], w)
        total = part if total is None else total + part
        o_ref[row // 2, :, cols] = dot(a_ref[...], w, NT).astype(BF16)
    ga_ref[...] = total.astype(ga_ref.dtype)


def output_of(t, attended, grads, steps, own, other, before=()):
    rows, cols = attended.shape
    groups, _, width = grads.shape
    first = not before
    chips = 4
    out = (
        jax.ShapeDtypeStruct((groups, rows, width), BF16),
        jax.ShapeDtypeStruct((rows, cols), F32 if first else BF16),
    )
    return pl.pallas_call(
        functools.partial(output_kernel, steps, first),
        out_shape=out,
        grid=(1,),
        in_specs=[
            SMEM,
            whole((rows, cols)),
            pl.BlockSpec((groups, rows, width), lambda i: (0, 1, 0)),
        ]
        + [ANY] * (len(own) + len(other))
        + [whole(b.shape) for b in before],
        out_specs=[whole(o.shape) for o in out],
        scratch_shapes=[
            pltpu.VMEM((len(steps), chips, 2, *own[0].shape[1:]), BF16),
            pltpu.SemaphoreType.DMA((len(steps), 2 * chips)),
        ],
        compiler_params=params(28),
        cost_estimate=cost(2 * rows * len(steps) * width * cols, len(steps) * width * cols),
        name="output",
    )(t, attended, grads, *own, *other, *before)


def backward_kernel(
    scale, t_ref, ga_ref, q_ref, k_ref, v_ref, p_ref, kw_ref, vw_ref, gq_ref, s0, s1, s2, s3, gk, gv, acc
):
    j, last = pl.program_id(0), pl.num_programs(0) - 1
    spans = q_ref.shape[0] // SPAN
    keys = k_ref.shape[0] // spans
    for h in range(q_ref.shape[1] // HEAD):
        c = slice(h * HEAD, (h + 1) * HEAD)
        for s in range(spans):
            qs = slice(s * SPAN, (s + 1) * SPAN)
            ks = slice(s * keys, (s + 1) * keys)
            probs, ga = p_ref[h, s], ga_ref[qs, c]
            gp = dot(ga, v_ref[ks, c], NT)
            inner = jnp.sum(probs * gp, axis=-1, keepdims=True)
            gs = (probs * (gp - inner) * scale).astype(BF16)
            gq_ref[qs, c] = dot(gs, k_ref[ks, c]).astype(BF16)
            gk[ks, c] = dot(gs, q_ref[qs, c], TN).astype(BF16)
            gv[ks, c] = dot(probs.astype(BF16), ga, TN).astype(BF16)
    part = dot(kw_ref[...], gk[...], NT) + dot(vw_ref[...], gv[...], NT)

    @pl.when(j == 0)
    def _():
        acc[...] = part

    @pl.when(j > 0)
    def _():
        acc[...] += part

    @pl.when(j == last)
    def _():
        blocks, rows, length = s0.shape
        for r, out in enumerate((s0, s1, s2, s3)):
            at = pl.multiple_of(((t_ref[0] + r) % 4) * rows, rows)
            for b in range(blocks):
                out[b] = acc[pl.ds(at, rows), b * length : (b + 1) * length].astype(BF16)


def backward_of(t, ga, query, key, value, probs, key_weight, value_weight, piece):
    rows, cols = query.shape
    tokens, width = key.shape[0], key_weight.shape[0]
    spans = rows // SPAN
    step = 2 * HEAD
    col = lambda n: pl.BlockSpec((n, step), lambda j, t: (0, j))
    return pl.pallas_call(
        functools.partial(backward_kernel, 1.0 / math.sqrt(HEAD)),
        out_shape=[jax.ShapeDtypeStruct((rows, cols), BF16)] + [jax.ShapeDtypeStruct(piece, BF16)] * 4,
        grid_spec=pltpu.PrefetchScalarGridSpec(
            num_scalar_prefetch=1,
            grid=(cols // step,),
            in_specs=[
                col(rows),
                col(rows),
                col(tokens),
                col(tokens),
                pl.BlockSpec((2, spans, SPAN, tokens // spans), lambda j, t: (j, 0, 0, 0)),
                col(width),
                col(width),
            ],
            out_specs=[col(rows)] + [whole(piece)] * 4,
            scratch_shapes=[
                pltpu.VMEM((tokens, step), BF16),
                pltpu.VMEM((tokens, step), BF16),
                pltpu.VMEM((width, tokens), F32),
            ],
        ),
        compiler_params=params(56),
        cost_estimate=cost(4 * tokens * width * cols, 10e6),
        name="backward",
    )(t, ga, query, key, value, probs, key_weight, value_weight)


def hidden_kernel(g_ref, w_ref, o_ref):
    o_ref[0] = dot(g_ref[...], w_ref[...], NT).astype(BF16)


def hidden_of(grad_query, weight):
    rows, cols = grad_query.shape
    width = weight.shape[0] // 4
    return pl.pallas_call(
        hidden_kernel,
        out_shape=jax.ShapeDtypeStruct((4, rows, width), BF16),
        grid=(4,),
        in_specs=[whole((rows, cols)), pl.BlockSpec((width, cols), lambda i: (i, 0))],
        out_specs=pl.BlockSpec((1, rows, width), lambda i: (i, 0, 0)),
        compiler_params=params(56),
        cost_estimate=cost(2 * rows * 4 * width * cols, 8 * width * cols),
        name="hidden",
    )(grad_query, weight)


def pairs_moved(blocks, gaps, sign):
    n = math.prod(lax.axis_size(a) for a in DP)
    pairs = blocks[:2], blocks[2:]
    got = [None, None]
    for by in range(1, WINDOW + 1):
        sent = jnp.where(gaps[0] == by, *pairs)
        came = lax.ppermute(sent, DP, [(i, (i + sign * by) % n) for i in range(n)])
        got = [came if g is None else jnp.where(gaps[k] == by, came, g) for k, g in enumerate(got)]
    return jnp.concatenate(got, axis=0)


def shifted(x, axis, by):
    n = lax.axis_size(axis)
    return lax.ppermute(x, axis, [(i, (i + by) % n) for i in range(n)])


def swapped(x):
    return lax.ppermute(x, "core", [(0, 1), (1, 0)])


def plane_blocks(rows):
    block = jnp.stack([rows] + [shifted(rows, "x", s) for s in range(1, lax.axis_size("x"))])
    up, down = [block], [block]
    for _ in range(lax.axis_size("z") // 2 - 1):
        up.append(shifted(up[-1], "z", 1))
        down.append(shifted(down[-1], "z", -1))
    half = block.shape[0] // 2
    far = shifted(up[-1][:half], "z", 1), shifted(down[-1][half:], "z", -1)
    return up, down, far


def shards(
    hidden,
    grad_out,
    query_weight,
    key_weight,
    value_weight,
    out_weight,
    neighbour_states,
    block_owner,
    slot_target,
):
    n_dp = math.prod(lax.axis_size(a) for a in DP)
    t = jnp.stack([lax.axis_index(a) for a in ("tensor", "core", "x", "z")]).astype(jnp.int32)
    up, down, far = plane_blocks(out_weight.T)
    early = [up[0], up[1], down[1], up[2], down[2]]
    late = [up[3], down[3], *far]

    gap = (block_owner[0] - lax.axis_index(DP) + n_dp) % n_dp
    gaps = (gap[0], gap[2])
    both = jnp.concatenate([hidden, grad_out], axis=0)
    pieces = exchanged(jnp.broadcast_to(both, (lax.axis_size("tensor"), *both.shape)))
    pieces = pieces.reshape(-1, *both.shape)
    mine = pairs_moved(jnp.swapaxes(neighbour_states, 1, 2), gaps, -1)
    neighbours = from_peers(mine)

    query = query_of(pieces, query_weight)
    key, value, probs, attended = forward_of(t, query, neighbours, key_weight, value_weight)
    steps = [(0, [0]), (-1, [0]), (1, [0]), (-2, [0]), (2, [0])], [(-3, [0]), (3, [0]), (4, [0, 2])]
    before = output_of(t, attended, pieces, steps[0], early, [swapped(b) for b in early])
    out_parts, grad_attended = output_of(
        t, attended, pieces, steps[1], late, [swapped(b) for b in late], before
    )
    cross_out = summed(exchanged(out_parts))
    grad_query, *state_parts = backward_of(
        t, grad_attended, query, key, value, probs, key_weight, value_weight, mine.shape
    )
    grad_hidden = summed(exchanged(tied(hidden_of(grad_query, query_weight), cross_out)))
    grads = summed(to_peers(state_parts))
    grad_states = jnp.swapaxes(pairs_moved(grads, gaps, 1), 1, 2)
    return cross_out, grad_hidden, grad_states


def solution(mesh):
    grid = Mesh(mesh.devices.reshape(8, 4, 2, 4), DP + ("tensor",))
    placed = (
        P(DP, "tensor"),
        P(DP, "tensor"),
        P(None, "tensor"),
        P(None, "tensor"),
        P(None, "tensor"),
        P("tensor", DP),
        P(DP, None, "tensor"),
        P(DP, None),
        P(DP, None),
    )
    return jax.shard_map(
        shards,
        mesh=grid,
        in_specs=placed,
        out_specs=(P(DP, "tensor"), P(DP, "tensor"), P(DP, None, "tensor")),
        check_vma=False,
    )
```

```python
import functools
import math

import jax
import jax.numpy as jnp
from jax import lax
from jax.experimental import pallas as pl
from jax.experimental.pallas import tpu as pltpu
from jax.sharding import Mesh, PartitionSpec as P

HEAD = 128
SPAN = 64
NBR = 128
WINDOW = 4
DP = ("z", "x", "core")
MIB = 1024 * 1024
F32, BF16 = jnp.float32, jnp.bfloat16

NN = (((1,), (0,)), ((), ()))
NT = (((1,), (1,)), ((), ()))
TN = (((0,), (0,)), ((), ()))


def dot(a, b, dims=NN):
    return lax.dot_general(a, b, dims, preferred_element_type=F32)


def params(mib):
    return pltpu.CompilerParams(vmem_limit_bytes=mib * MIB)


ANY = pl.BlockSpec(memory_space=pl.ANY)
SMEM = pl.BlockSpec(memory_space=pltpu.SMEM)


def whole(shape):
    return pl.BlockSpec(shape, lambda *_: (0,) * len(shape))


def cost(flops, nbytes):
    return pl.CostEstimate(flops=int(flops), bytes_accessed=int(nbytes), transcendentals=0)


def from_peers(x):
    n = lax.axis_size("tensor")
    got = [x]
    for r in range(1, n):
        got.append(lax.ppermute(x, "tensor", [((i + r) % n, i) for i in range(n)]))
    return got


def to_peers(pieces):
    n = lax.axis_size("tensor")
    got = [pieces[0]]
    for r in range(1, n):
        got.append(lax.ppermute(pieces[r], "tensor", [(i, (i + r) % n) for i in range(n)]))
    return got


def exchanged(x):
    return lax.all_to_all(x, "tensor", split_axis=0, concat_axis=0, tiled=True)


def summed(parts):
    total = parts[0].astype(F32)
    for part in parts[1:]:
        total = total + part.astype(F32)
    return total.astype(BF16)


def nothing(*_):
    pass


def tied(x, *after):
    return pl.pallas_call(
        nothing,
        out_shape=jax.ShapeDtypeStruct(x.shape, x.dtype),
        in_specs=[ANY] * (1 + len(after)),
        out_specs=ANY,
        input_output_aliases={0: 0},
        compiler_params=params(1),
        name="tied",
    )(x, *after)


def query_kernel(h_ref, w_ref, q_ref, acc):
    i, last = pl.program_id(0), pl.num_programs(0) - 1
    part = dot(h_ref[0], w_ref[...])

    @pl.when(i == 0)
    def _():
        acc[...] = part

    @pl.when(jnp.logical_and(i > 0, i < last))
    def _():
        acc[...] += part

    @pl.when(i == last)
    def _():
        q_ref[...] = (acc[...] + part).astype(BF16)


def query_of(pieces, weight):
    steps, rows, width = pieces.shape
    rows, cols = rows // 2, weight.shape[1]
    return pl.pallas_call(
        query_kernel,
        out_shape=jax.ShapeDtypeStruct((rows, cols), BF16),
        grid=(steps,),
        in_specs=[
            pl.BlockSpec((1, rows, width), lambda i: (i, 0, 0)),
            pl.BlockSpec((width, cols), lambda i: (i, 0)),
        ],
        out_specs=whole((rows, cols)),
        scratch_shapes=[pltpu.VMEM((rows, cols), F32)],
        compiler_params=params(56),
        cost_estimate=cost(2 * rows * steps * width * cols, 2 * steps * width * cols),
        name="query",
    )(pieces, weight)


def forward_kernel(
    scale, t_ref, q_ref, n0, n1, n2, n3, kw_ref, vw_ref, k_ref, v_ref, p_ref, a_ref, flipped, rows
):
    blocks, part, length = n0.shape

    @pl.when(pl.program_id(0) == 0)
    def _():
        for r, n in enumerate((n0, n1, n2, n3)):
            at = pl.multiple_of(((t_ref[0] + r) % 4) * part, part)
            for b in range(blocks):
                flipped[pl.ds(at, part), b * length : (b + 1) * length] = n[b]
        rows[...] = flipped[...].T

    k_ref[...] = dot(rows[...], kw_ref[...]).astype(BF16)
    v_ref[...] = dot(rows[...], vw_ref[...]).astype(BF16)
    spans = q_ref.shape[0] // SPAN
    keys = k_ref.shape[0] // spans
    for j in range(q_ref.shape[1] // HEAD):
        c = slice(j * HEAD, (j + 1) * HEAD)
        for s in range(spans):
            qs = slice(s * SPAN, (s + 1) * SPAN)
            ks = slice(s * keys, (s + 1) * keys)
            scores = dot(q_ref[qs, c], k_ref[ks, c], NT) * scale
            e = jnp.exp(scores - jnp.max(scores, axis=-1, keepdims=True))
            probs = e / jnp.sum(e, axis=-1, keepdims=True)
            p_ref[j, s] = probs
            a_ref[qs, c] = dot(probs.astype(BF16), v_ref[ks, c]).astype(BF16)


def forward_of(t, query, pieces, key_weight, value_weight):
    rows, cols = query.shape
    blocks, part, length = pieces[0].shape
    tokens, width = blocks * length, key_weight.shape[0]
    spans = rows // SPAN
    step = 2 * HEAD
    col = lambda n: pl.BlockSpec((n, step), lambda j, t: (0, j))
    return pl.pallas_call(
        functools.partial(forward_kernel, 1.0 / math.sqrt(HEAD)),
        out_shape=(
            jax.ShapeDtypeStruct((tokens, cols), BF16),
            jax.ShapeDtypeStruct((tokens, cols), BF16),
            jax.ShapeDtypeStruct((cols // HEAD, spans, SPAN, tokens // spans), F32),
            jax.ShapeDtypeStruct((rows, cols), BF16),
        ),
        grid_spec=pltpu.PrefetchScalarGridSpec(
            num_scalar_prefetch=1,
            grid=(cols // step,),
            in_specs=[col(rows)] + [whole(pieces[0].shape)] * 4 + [col(width)] * 2,
            out_specs=[
                col(tokens),
                col(tokens),
                pl.BlockSpec((2, spans, SPAN, tokens // spans), lambda j, t: (j, 0, 0, 0)),
                col(rows),
            ],
            scratch_shapes=[pltpu.VMEM((width, tokens), BF16), pltpu.VMEM((tokens, width), BF16)],
        ),
        compiler_params=params(56),
        cost_estimate=cost(4 * tokens * width * cols, 10e6),
        name="forward",
    )(t, query, *pieces, key_weight, value_weight)


def output_kernel(steps, first, t_ref, a_ref, g_ref, *refs):
    pieces = sum(len(firsts) for _, firsts in steps)
    own, other, refs = refs[:pieces], refs[pieces : 2 * pieces], refs[2 * pieces :]
    if not first:
        o_before, ga_before, *refs = refs
    o_ref, ga_ref, w_ref, sems = refs
    core, x, z = t_ref[1], t_ref[2], t_ref[3]
    chips, deep = w_ref.shape[1], 2 * g_ref.shape[0]
    width = g_ref.shape[2] // 2
    groups = []
    n = 0
    for i, (_, firsts) in enumerate(steps):
        copies = []
        for start in firsts:
            for s in range(own[n].shape[0]):
                at = (x - start - s + chips) % chips
                for plane, c in ((own[n], core), (other[n], 1 - core)):
                    copies.append(
                        pltpu.make_async_copy(plane.at[s], w_ref.at[i, at, c], sems.at[i, len(copies)])
                    )
            n += 1
        groups.append(copies)
    for copies in groups:
        for copy in copies:
            copy.start()
    total = None if first else ga_before[...]
    if not first:
        o_ref[...] = o_before[...]
    for i, (step, _) in enumerate(steps):
        for copy in groups[i]:
            copy.wait()
        w = w_ref[i].reshape(width, a_ref.shape[1])
        row = (z + step + deep) % deep
        cols = pl.ds(pl.multiple_of((row % 2) * width, width), width)
        part = dot(g_ref[row // 2, :, cols], w)
        total = part if total is None else total + part
        o_ref[row // 2, :, cols] = dot(a_ref[...], w, NT).astype(BF16)
    ga_ref[...] = total.astype(ga_ref.dtype)


def output_of(t, attended, grads, steps, own, other, before=()):
    rows, cols = attended.shape
    groups, _, width = grads.shape
    first = not before
    chips = 4
    out = (
        jax.ShapeDtypeStruct((groups, rows, width), BF16),
        jax.ShapeDtypeStruct((rows, cols), F32 if first else BF16),
    )
    return pl.pallas_call(
        functools.partial(output_kernel, steps, first),
        out_shape=out,
        grid=(1,),
        in_specs=[
            SMEM,
            whole((rows, cols)),
            pl.BlockSpec((groups, rows, width), lambda i: (0, 1, 0)),
        ]
        + [ANY] * (len(own) + len(other))
        + [whole(b.shape) for b in before],
        out_specs=[whole(o.shape) for o in out],
        scratch_shapes=[
            pltpu.VMEM((len(steps), chips, 2, *own[0].shape[1:]), BF16),
            pltpu.SemaphoreType.DMA((len(steps), 2 * chips)),
        ],
        compiler_params=params(28),
        cost_estimate=cost(2 * rows * len(steps) * width * cols, len(steps) * width * cols),
        name="output",
    )(t, attended, grads, *own, *other, *before)


def backward_kernel(
    scale, t_ref, ga_ref, q_ref, k_ref, v_ref, p_ref, kw_ref, vw_ref, gq_ref, s0, s1, s2, s3, gk, gv, acc
):
    j, last = pl.program_id(0), pl.num_programs(0) - 1
    spans = q_ref.shape[0] // SPAN
    keys = k_ref.shape[0] // spans
    for h in range(q_ref.shape[1] // HEAD):
        c = slice(h * HEAD, (h + 1) * HEAD)
        for s in range(spans):
            qs = slice(s * SPAN, (s + 1) * SPAN)
            ks = slice(s * keys, (s + 1) * keys)
            probs, ga = p_ref[h, s], ga_ref[qs, c]
            gp = dot(ga, v_ref[ks, c], NT)
            inner = jnp.sum(probs * gp, axis=-1, keepdims=True)
            gs = (probs * (gp - inner) * scale).astype(BF16)
            gq_ref[qs, c] = dot(gs, k_ref[ks, c]).astype(BF16)
            gk[ks, c] = dot(gs, q_ref[qs, c], TN).astype(BF16)
            gv[ks, c] = dot(probs.astype(BF16), ga, TN).astype(BF16)
    part = dot(kw_ref[...], gk[...], NT) + dot(vw_ref[...], gv[...], NT)

    @pl.when(j == 0)
    def _():
        acc[...] = part

    @pl.when(j > 0)
    def _():
        acc[...] += part

    @pl.when(j == last)
    def _():
        blocks, rows, length = s0.shape
        for r, out in enumerate((s0, s1, s2, s3)):
            at = pl.multiple_of(((t_ref[0] + r) % 4) * rows, rows)
            for b in range(blocks):
                out[b] = acc[pl.ds(at, rows), b * length : (b + 1) * length].astype(BF16)


def backward_of(t, ga, query, key, value, probs, key_weight, value_weight, piece):
    rows, cols = query.shape
    tokens, width = key.shape[0], key_weight.shape[0]
    spans = rows // SPAN
    step = 2 * HEAD
    col = lambda n: pl.BlockSpec((n, step), lambda j, t: (0, j))
    return pl.pallas_call(
        functools.partial(backward_kernel, 1.0 / math.sqrt(HEAD)),
        out_shape=[jax.ShapeDtypeStruct((rows, cols), BF16)] + [jax.ShapeDtypeStruct(piece, BF16)] * 4,
        grid_spec=pltpu.PrefetchScalarGridSpec(
            num_scalar_prefetch=1,
            grid=(cols // step,),
            in_specs=[
                col(rows),
                col(rows),
                col(tokens),
                col(tokens),
                pl.BlockSpec((2, spans, SPAN, tokens // spans), lambda j, t: (j, 0, 0, 0)),
                col(width),
                col(width),
            ],
            out_specs=[col(rows)] + [whole(piece)] * 4,
            scratch_shapes=[
                pltpu.VMEM((tokens, step), BF16),
                pltpu.VMEM((tokens, step), BF16),
                pltpu.VMEM((width, tokens), F32),
            ],
        ),
        compiler_params=params(56),
        cost_estimate=cost(4 * tokens * width * cols, 10e6),
        name="backward",
    )(t, ga, query, key, value, probs, key_weight, value_weight)


def hidden_kernel(g_ref, w_ref, o_ref):
    o_ref[0] = dot(g_ref[...], w_ref[...], NT).astype(BF16)


def hidden_of(grad_query, weight):
    rows, cols = grad_query.shape
    width = weight.shape[0] // 4
    return pl.pallas_call(
        hidden_kernel,
        out_shape=jax.ShapeDtypeStruct((4, rows, width), BF16),
        grid=(4,),
        in_specs=[whole((rows, cols)), pl.BlockSpec((width, cols), lambda i: (i, 0))],
        out_specs=pl.BlockSpec((1, rows, width), lambda i: (i, 0, 0)),
        compiler_params=params(56),
        cost_estimate=cost(2 * rows * 4 * width * cols, 8 * width * cols),
        name="hidden",
    )(grad_query, weight)


def pairs_moved(blocks, gaps, sign):
    n = math.prod(lax.axis_size(a) for a in DP)
    pairs = blocks[:2], blocks[2:]
    got = [None, None]
    for by in range(1, WINDOW + 1):
        sent = jnp.where(gaps[0] == by, *pairs)
        came = lax.ppermute(sent, DP, [(i, (i + sign * by) % n) for i in range(n)])
        got = [came if g is None else jnp.where(gaps[k] == by, came, g) for k, g in enumerate(got)]
    return jnp.concatenate(got, axis=0)


def shifted(x, axis, by):
    n = lax.axis_size(axis)
    return lax.ppermute(x, axis, [(i, (i + by) % n) for i in range(n)])


def swapped(x):
    return lax.ppermute(x, "core", [(0, 1), (1, 0)])


def plane_blocks(rows):
    block = jnp.stack([rows] + [shifted(rows, "x", s) for s in range(1, lax.axis_size("x"))])
    up, down = [block], [block]
    for _ in range(lax.axis_size("z") // 2 - 1):
        up.append(shifted(up[-1], "z", 1))
        down.append(shifted(down[-1], "z", -1))
    return up, down


def far_pieces(up, down, *after):
    half = up.shape[0] // 2
    return shifted(tied(up[:half], *after), "z", 1), shifted(tied(down[half:], *after), "z", -1)


def shards(
    hidden,
    grad_out,
    query_weight,
    key_weight,
    value_weight,
    out_weight,
    neighbour_states,
    block_owner,
    slot_target,
):
    n_dp = math.prod(lax.axis_size(a) for a in DP)
    t = jnp.stack([lax.axis_index(a) for a in ("tensor", "core", "x", "z")]).astype(jnp.int32)
    up, down = plane_blocks(out_weight.T)
    early = [up[0], up[1], down[1], up[2], down[2]]

    gap = (block_owner[0] - lax.axis_index(DP) + n_dp) % n_dp
    gaps = (gap[0], gap[2])
    both = jnp.concatenate([hidden, grad_out], axis=0)
    pieces = exchanged(jnp.broadcast_to(both, (lax.axis_size("tensor"), *both.shape)))
    pieces = pieces.reshape(-1, *both.shape)
    mine = pairs_moved(jnp.swapaxes(neighbour_states, 1, 2), gaps, -1)
    neighbours = from_peers(mine)

    query = query_of(pieces, query_weight)
    key, value, probs, attended = forward_of(t, query, neighbours, key_weight, value_weight)
    late = [up[3], down[3], *far_pieces(up[3], down[3], attended)]
    steps = [(0, [0]), (-1, [0]), (1, [0]), (-2, [0]), (2, [0])], [(-3, [0]), (3, [0]), (4, [0, 2])]
    before = output_of(t, attended, pieces, steps[0], early, [swapped(b) for b in early])
    out_parts, grad_attended = output_of(
        t, attended, pieces, steps[1], late, [swapped(b) for b in late], before
    )
    cross_out = summed(exchanged(out_parts))
    grad_query, *state_parts = backward_of(
        t, grad_attended, query, key, value, probs, key_weight, value_weight, mine.shape
    )
    grad_hidden = summed(exchanged(tied(hidden_of(grad_query, query_weight), cross_out)))
    grads = summed(to_peers(state_parts))
    grad_states = jnp.swapaxes(pairs_moved(grads, gaps, 1), 1, 2)
    return cross_out, grad_hidden, grad_states


def solution(mesh):
    grid = Mesh(mesh.devices.reshape(8, 4, 2, 4), DP + ("tensor",))
    placed = (
        P(DP, "tensor"),
        P(DP, "tensor"),
        P(None, "tensor"),
        P(None, "tensor"),
        P(None, "tensor"),
        P("tensor", DP),
        P(DP, None, "tensor"),
        P(DP, None),
        P(DP, None),
    )
    return jax.shard_map(
        shards,
        mesh=grid,
        in_specs=placed,
        out_specs=(P(DP, "tensor"), P(DP, "tensor"), P(DP, None, "tensor")),
        check_vma=False,
    )
```

```python
import functools
import math

import jax
import jax.numpy as jnp
from jax import lax
from jax.experimental import pallas as pl
from jax.experimental.pallas import tpu as pltpu
from jax.sharding import Mesh, PartitionSpec as P

HEAD = 128
SPAN = 64
NBR = 128
WINDOW = 4
DP = ("z", "x", "core")
MIB = 1024 * 1024
F32, BF16 = jnp.float32, jnp.bfloat16

NN = (((1,), (0,)), ((), ()))
NT = (((1,), (1,)), ((), ()))
TN = (((0,), (0,)), ((), ()))


def dot(a, b, dims=NN):
    return lax.dot_general(a, b, dims, preferred_element_type=F32)


def params(mib):
    return pltpu.CompilerParams(vmem_limit_bytes=mib * MIB)


ANY = pl.BlockSpec(memory_space=pl.ANY)
SMEM = pl.BlockSpec(memory_space=pltpu.SMEM)


def whole(shape):
    return pl.BlockSpec(shape, lambda *_: (0,) * len(shape))


def cost(flops, nbytes):
    return pl.CostEstimate(flops=int(flops), bytes_accessed=int(nbytes), transcendentals=0)


def from_peers(x):
    n = lax.axis_size("tensor")
    got = [x]
    for r in range(1, n):
        got.append(lax.ppermute(x, "tensor", [((i + r) % n, i) for i in range(n)]))
    return got


def to_peers(pieces):
    n = lax.axis_size("tensor")
    got = [pieces[0]]
    for r in range(1, n):
        got.append(lax.ppermute(pieces[r], "tensor", [(i, (i + r) % n) for i in range(n)]))
    return got


def exchanged(x):
    return lax.all_to_all(x, "tensor", split_axis=0, concat_axis=0, tiled=True)


def summed(parts):
    total = parts[0].astype(F32)
    for part in parts[1:]:
        total = total + part.astype(F32)
    return total.astype(BF16)


def nothing(*_):
    pass


def tied(x, *after):
    return pl.pallas_call(
        nothing,
        out_shape=jax.ShapeDtypeStruct(x.shape, x.dtype),
        in_specs=[ANY] * (1 + len(after)),
        out_specs=ANY,
        input_output_aliases={0: 0},
        name="tied",
    )(x, *after)


def query_kernel(h_ref, w_ref, q_ref, acc):
    i, last = pl.program_id(0), pl.num_programs(0) - 1
    part = dot(h_ref[0], w_ref[...])

    @pl.when(i == 0)
    def _():
        acc[...] = part

    @pl.when(jnp.logical_and(i > 0, i < last))
    def _():
        acc[...] += part

    @pl.when(i == last)
    def _():
        q_ref[...] = (acc[...] + part).astype(BF16)


def query_of(pieces, weight):
    steps, rows, width = pieces.shape
    rows, cols = rows // 2, weight.shape[1]
    return pl.pallas_call(
        query_kernel,
        out_shape=jax.ShapeDtypeStruct((rows, cols), BF16),
        grid=(steps,),
        in_specs=[
            pl.BlockSpec((1, rows, width), lambda i: (i, 0, 0)),
            pl.BlockSpec((width, cols), lambda i: (i, 0)),
        ],
        out_specs=whole((rows, cols)),
        scratch_shapes=[pltpu.VMEM((rows, cols), F32)],
        compiler_params=params(56),
        cost_estimate=cost(2 * rows * steps * width * cols, 2 * steps * width * cols),
        name="query",
    )(pieces, weight)


def forward_kernel(
    scale, t_ref, q_ref, n0, n1, n2, n3, kw_ref, vw_ref, k_ref, v_ref, p_ref, a_ref, flipped, rows
):
    blocks, part, length = n0.shape

    @pl.when(pl.program_id(0) == 0)
    def _():
        for r, n in enumerate((n0, n1, n2, n3)):
            at = pl.multiple_of(((t_ref[0] + r) % 4) * part, part)
            for b in range(blocks):
                flipped[pl.ds(at, part), b * length : (b + 1) * length] = n[b]
        rows[...] = flipped[...].T

    k_ref[...] = dot(rows[...], kw_ref[...]).astype(BF16)
    v_ref[...] = dot(rows[...], vw_ref[...]).astype(BF16)
    spans = q_ref.shape[0] // SPAN
    keys = k_ref.shape[0] // spans
    for j in range(q_ref.shape[1] // HEAD):
        c = slice(j * HEAD, (j + 1) * HEAD)
        for s in range(spans):
            qs = slice(s * SPAN, (s + 1) * SPAN)
            ks = slice(s * keys, (s + 1) * keys)
            scores = dot(q_ref[qs, c], k_ref[ks, c], NT) * scale
            e = jnp.exp(scores - jnp.max(scores, axis=-1, keepdims=True))
            probs = e / jnp.sum(e, axis=-1, keepdims=True)
            p_ref[j, s] = probs
            a_ref[qs, c] = dot(probs.astype(BF16), v_ref[ks, c]).astype(BF16)


def forward_of(t, query, pieces, key_weight, value_weight):
    rows, cols = query.shape
    blocks, part, length = pieces[0].shape
    tokens, width = blocks * length, key_weight.shape[0]
    spans = rows // SPAN
    step = 2 * HEAD
    col = lambda n: pl.BlockSpec((n, step), lambda j, t: (0, j))
    return pl.pallas_call(
        functools.partial(forward_kernel, 1.0 / math.sqrt(HEAD)),
        out_shape=(
            jax.ShapeDtypeStruct((tokens, cols), BF16),
            jax.ShapeDtypeStruct((tokens, cols), BF16),
            jax.ShapeDtypeStruct((cols // HEAD, spans, SPAN, tokens // spans), F32),
            jax.ShapeDtypeStruct((rows, cols), BF16),
        ),
        grid_spec=pltpu.PrefetchScalarGridSpec(
            num_scalar_prefetch=1,
            grid=(cols // step,),
            in_specs=[col(rows)] + [whole(pieces[0].shape)] * 4 + [col(width)] * 2,
            out_specs=[
                col(tokens),
                col(tokens),
                pl.BlockSpec((2, spans, SPAN, tokens // spans), lambda j, t: (j, 0, 0, 0)),
                col(rows),
            ],
            scratch_shapes=[pltpu.VMEM((width, tokens), BF16), pltpu.VMEM((tokens, width), BF16)],
        ),
        compiler_params=params(56),
        cost_estimate=cost(4 * tokens * width * cols, 10e6),
        name="forward",
    )(t, query, *pieces, key_weight, value_weight)


def output_kernel(first, t_ref, a_ref, g_ref, w_ref, *refs):
    if not first:
        o_before, ga_before, *refs = refs
    o_ref, ga_ref, pick, acc = refs
    i, last = pl.program_id(0), pl.num_programs(0) - 1
    deep, chips, group, cols = w_ref.shape
    rows, width = g_ref.shape[1], chips * group

    @pl.when(i == 0)
    def _():
        core = t_ref[1] if first else 1 - t_ref[1]
        full = lax.broadcasted_iota(jnp.int32, pick.shape, 0)
        part = lax.broadcasted_iota(jnp.int32, pick.shape, 1)
        chip = (t_ref[2] - part // group + chips) % chips
        pick[...] = jnp.where(full == chip * 2 * group + core * group + part % group, 1.0, 0.0).astype(BF16)
        acc[...] = jnp.zeros_like(acc) if first else ga_before[...]

    both = jnp.concatenate([g_ref[0, :, : 2 * width], g_ref[0, :, 2 * width :]], axis=0)
    picked = dot(both, pick[...]).astype(BF16)
    total, outs = acc[...], []
    for z in range(deep):
        w = w_ref[z].reshape(width, cols)
        total = total + dot(picked[z * rows : (z + 1) * rows], w)
        outs.append(dot(a_ref[...], w, NT).astype(BF16))
    acc[...] = total
    placed = dot(jnp.concatenate(outs, axis=0), pick[...], NT)
    for z in range(deep):
        at = slice(z * 2 * width, (z + 1) * 2 * width)
        out = placed[z * rows : (z + 1) * rows]
        o_ref[0, :, at] = (out if first else out + o_before[0, :, at].astype(F32)).astype(BF16)

    @pl.when(i == last)
    def _():
        ga_ref[...] = total.astype(ga_ref.dtype)


def output_of(t, attended, pieces, plane, before=()):
    rows, cols = attended.shape
    steps, _, width = pieces.shape
    first = not before
    block = pl.BlockSpec((1, rows, width), lambda i: (i, 0, 0))
    deep = plane.shape[0] // steps
    return pl.pallas_call(
        functools.partial(output_kernel, first),
        out_shape=(
            jax.ShapeDtypeStruct((steps, rows, width), BF16),
            jax.ShapeDtypeStruct((rows, cols), F32 if first else BF16),
        ),
        grid=(steps,),
        in_specs=[
            SMEM,
            whole((rows, cols)),
            pl.BlockSpec((1, rows, width), lambda i: (i, 1, 0)),
            pl.BlockSpec((deep, *plane.shape[1:]), lambda i: (i, 0, 0, 0)),
        ]
        + ([] if first else [block, whole((rows, cols))]),
        out_specs=(block, whole((rows, cols))),
        scratch_shapes=[
            pltpu.VMEM((width // deep, width // deep // 2), BF16),
            pltpu.VMEM((rows, cols), F32),
        ],
        compiler_params=params(28),
        cost_estimate=cost(2 * rows * steps * width * cols, steps * width * cols),
        name="output",
    )(t, attended, pieces, plane, *before)


def backward_kernel(
    scale, t_ref, ga_ref, q_ref, k_ref, v_ref, p_ref, kw_ref, vw_ref, gq_ref, s0, s1, s2, s3, gk, gv, acc
):
    j, last = pl.program_id(0), pl.num_programs(0) - 1
    spans = q_ref.shape[0] // SPAN
    keys = k_ref.shape[0] // spans
    for h in range(q_ref.shape[1] // HEAD):
        c = slice(h * HEAD, (h + 1) * HEAD)
        for s in range(spans):
            qs = slice(s * SPAN, (s + 1) * SPAN)
            ks = slice(s * keys, (s + 1) * keys)
            probs, ga = p_ref[h, s], ga_ref[qs, c]
            gp = dot(ga, v_ref[ks, c], NT)
            inner = jnp.sum(probs * gp, axis=-1, keepdims=True)
            gs = (probs * (gp - inner) * scale).astype(BF16)
            gq_ref[qs, c] = dot(gs, k_ref[ks, c]).astype(BF16)
            gk[ks, c] = dot(gs, q_ref[qs, c], TN).astype(BF16)
            gv[ks, c] = dot(probs.astype(BF16), ga, TN).astype(BF16)
    part = dot(kw_ref[...], gk[...], NT) + dot(vw_ref[...], gv[...], NT)

    @pl.when(j == 0)
    def _():
        acc[...] = part

    @pl.when(j > 0)
    def _():
        acc[...] += part

    @pl.when(j == last)
    def _():
        blocks, rows, length = s0.shape
        for r, out in enumerate((s0, s1, s2, s3)):
            at = pl.multiple_of(((t_ref[0] + r) % 4) * rows, rows)
            for b in range(blocks):
                out[b] = acc[pl.ds(at, rows), b * length : (b + 1) * length].astype(BF16)


def backward_of(t, ga, query, key, value, probs, key_weight, value_weight, piece):
    rows, cols = query.shape
    tokens, width = key.shape[0], key_weight.shape[0]
    spans = rows // SPAN
    step = 2 * HEAD
    col = lambda n: pl.BlockSpec((n, step), lambda j, t: (0, j))
    return pl.pallas_call(
        functools.partial(backward_kernel, 1.0 / math.sqrt(HEAD)),
        out_shape=[jax.ShapeDtypeStruct((rows, cols), BF16)] + [jax.ShapeDtypeStruct(piece, BF16)] * 4,
        grid_spec=pltpu.PrefetchScalarGridSpec(
            num_scalar_prefetch=1,
            grid=(cols // step,),
            in_specs=[
                col(rows),
                col(rows),
                col(tokens),
                col(tokens),
                pl.BlockSpec((2, spans, SPAN, tokens // spans), lambda j, t: (j, 0, 0, 0)),
                col(width),
                col(width),
            ],
            out_specs=[col(rows)] + [whole(piece)] * 4,
            scratch_shapes=[
                pltpu.VMEM((tokens, step), BF16),
                pltpu.VMEM((tokens, step), BF16),
                pltpu.VMEM((width, tokens), F32),
            ],
        ),
        compiler_params=params(56),
        cost_estimate=cost(4 * tokens * width * cols, 10e6),
        name="backward",
    )(t, ga, query, key, value, probs, key_weight, value_weight)


def hidden_kernel(g_ref, w_ref, o_ref):
    o_ref[0] = dot(g_ref[...], w_ref[...], NT).astype(BF16)


def hidden_of(grad_query, weight):
    rows, cols = grad_query.shape
    width = weight.shape[0] // 4
    return pl.pallas_call(
        hidden_kernel,
        out_shape=jax.ShapeDtypeStruct((4, rows, width), BF16),
        grid=(4,),
        in_specs=[whole((rows, cols)), pl.BlockSpec((width, cols), lambda i: (i, 0))],
        out_specs=pl.BlockSpec((1, rows, width), lambda i: (i, 0, 0)),
        compiler_params=params(56),
        cost_estimate=cost(2 * rows * 4 * width * cols, 8 * width * cols),
        name="hidden",
    )(grad_query, weight)


def pairs_moved(blocks, gaps, sign):
    n = math.prod(lax.axis_size(a) for a in DP)
    pairs = blocks[:2], blocks[2:]
    got = [None, None]
    for by in range(1, WINDOW + 1):
        sent = jnp.where(gaps[0] == by, *pairs)
        came = lax.ppermute(sent, DP, [(i, (i + sign * by) % n) for i in range(n)])
        got = [came if g is None else jnp.where(gaps[k] == by, came, g) for k, g in enumerate(got)]
    return jnp.concatenate(got, axis=0)


def gathered_plane(rows):
    n = lax.axis_size("x")
    along = [rows]
    for s in range(1, n):
        along.append(lax.ppermute(rows, "x", [(i, (i + s) % n) for i in range(n)]))
    return lax.all_gather(jnp.stack(along), "z", axis=0)


def shards(
    hidden,
    grad_out,
    query_weight,
    key_weight,
    value_weight,
    out_weight,
    neighbour_states,
    block_owner,
    slot_target,
):
    n_dp = math.prod(lax.axis_size(a) for a in DP)
    t = jnp.stack([lax.axis_index(a) for a in ("tensor", "core", "x")]).astype(jnp.int32)
    plane = gathered_plane(out_weight.T)

    gap = (block_owner[0] - lax.axis_index(DP) + n_dp) % n_dp
    gaps = (gap[0], gap[2])
    both = jnp.concatenate([hidden, grad_out], axis=0)
    pieces = exchanged(jnp.broadcast_to(both, (lax.axis_size("tensor"), *both.shape)))
    pieces = pieces.reshape(-1, *both.shape)
    mine = pairs_moved(jnp.swapaxes(neighbour_states, 1, 2), gaps, -1)
    neighbours = from_peers(mine)

    query = query_of(pieces, query_weight)
    key, value, probs, attended = forward_of(t, query, neighbours, key_weight, value_weight)
    plane = tied(plane, attended)
    other_plane = lax.ppermute(plane, "core", [(0, 1), (1, 0)])
    before = output_of(t, attended, pieces, plane)
    out_parts, grad_attended = output_of(t, attended, pieces, other_plane, before)
    cross_out = summed(exchanged(out_parts))
    grad_query, *state_parts = backward_of(
        t, grad_attended, query, key, value, probs, key_weight, value_weight, mine.shape
    )
    grad_hidden = summed(exchanged(hidden_of(grad_query, query_weight)))
    grads = summed(to_peers(state_parts))
    grad_states = jnp.swapaxes(pairs_moved(grads, gaps, 1), 1, 2)
    return cross_out, grad_hidden, grad_states


def solution(mesh):
    grid = Mesh(mesh.devices.reshape(8, 4, 2, 4), DP + ("tensor",))
    placed = (
        P(DP, "tensor"),
        P(DP, "tensor"),
        P(None, "tensor"),
        P(None, "tensor"),
        P(None, "tensor"),
        P("tensor", DP),
        P(DP, None, "tensor"),
        P(DP, None),
        P(DP, None),
    )
    return jax.shard_map(
        shards,
        mesh=grid,
        in_specs=placed,
        out_specs=(P(DP, "tensor"), P(DP, "tensor"), P(DP, None, "tensor")),
        check_vma=False,
    )
```

```python
import functools
import itertools
import math

import jax
import jax.numpy as jnp
from jax import lax
from jax.experimental import pallas as pl
from jax.experimental.pallas import tpu as pltpu
from jax.sharding import Mesh, PartitionSpec as P

HEAD = 128
SPAN = 64
NBR = 128
WINDOW = 4
DP = ("z", "x", "core")
MIB = 1024 * 1024
F32, BF16 = jnp.float32, jnp.bfloat16

NN = (((1,), (0,)), ((), ()))
NT = (((1,), (1,)), ((), ()))
TN = (((0,), (0,)), ((), ()))


def dot(a, b, dims=NN):
    return lax.dot_general(a, b, dims, preferred_element_type=F32)


def params(mib):
    return pltpu.CompilerParams(vmem_limit_bytes=mib * MIB)


ANY = pl.BlockSpec(memory_space=pl.ANY)
SMEM = pl.BlockSpec(memory_space=pltpu.SMEM)


def whole(shape):
    return pl.BlockSpec(shape, lambda *_: (0,) * len(shape))


def cost(flops, nbytes):
    return pl.CostEstimate(flops=int(flops), bytes_accessed=int(nbytes), transcendentals=0)


def from_peers(x):
    n = lax.axis_size("tensor")
    got = [x]
    for r in range(1, n):
        got.append(lax.ppermute(x, "tensor", [((i + r) % n, i) for i in range(n)]))
    return got


def to_peers(pieces):
    n = lax.axis_size("tensor")
    got = [pieces[0]]
    for r in range(1, n):
        got.append(lax.ppermute(pieces[r], "tensor", [(i, (i + r) % n) for i in range(n)]))
    return got


def exchanged(x):
    return lax.all_to_all(x, "tensor", split_axis=0, concat_axis=0, tiled=True)


def summed(parts):
    total = parts[0].astype(F32)
    for part in parts[1:]:
        total = total + part.astype(F32)
    return total.astype(BF16)


def nothing(*_):
    pass


def tied(x, *after):
    return pl.pallas_call(
        nothing,
        out_shape=jax.ShapeDtypeStruct(x.shape, x.dtype),
        in_specs=[ANY] * (1 + len(after)),
        out_specs=ANY,
        input_output_aliases={0: 0},
        name="tied",
    )(x, *after)


def query_kernel(h_ref, w_ref, q_ref, acc):
    i, last = pl.program_id(0), pl.num_programs(0) - 1
    part = dot(h_ref[0], w_ref[...])

    @pl.when(i == 0)
    def _():
        acc[...] = part

    @pl.when(jnp.logical_and(i > 0, i < last))
    def _():
        acc[...] += part

    @pl.when(i == last)
    def _():
        q_ref[...] = (acc[...] + part).astype(BF16)


def query_of(pieces, weight):
    steps, rows, width = pieces.shape
    rows, cols = rows // 2, weight.shape[1]
    return pl.pallas_call(
        query_kernel,
        out_shape=jax.ShapeDtypeStruct((rows, cols), BF16),
        grid=(steps,),
        in_specs=[
            pl.BlockSpec((1, rows, width), lambda i: (i, 0, 0)),
            pl.BlockSpec((width, cols), lambda i: (i, 0)),
        ],
        out_specs=whole((rows, cols)),
        scratch_shapes=[pltpu.VMEM((rows, cols), F32)],
        compiler_params=params(56),
        cost_estimate=cost(2 * rows * steps * width * cols, 2 * steps * width * cols),
        name="query",
    )(pieces, weight)


def forward_kernel(
    scale, t_ref, q_ref, n0, n1, n2, n3, kw_ref, vw_ref, k_ref, v_ref, p_ref, a_ref, flipped, rows
):
    blocks, part, length = n0.shape

    @pl.when(pl.program_id(0) == 0)
    def _():
        for r, n in enumerate((n0, n1, n2, n3)):
            at = pl.multiple_of(((t_ref[0] + r) % 4) * part, part)
            for b in range(blocks):
                flipped[pl.ds(at, part), b * length : (b + 1) * length] = n[b]
        rows[...] = flipped[...].T

    k_ref[...] = dot(rows[...], kw_ref[...]).astype(BF16)
    v_ref[...] = dot(rows[...], vw_ref[...]).astype(BF16)
    spans = q_ref.shape[0] // SPAN
    keys = k_ref.shape[0] // spans
    for j in range(q_ref.shape[1] // HEAD):
        c = slice(j * HEAD, (j + 1) * HEAD)
        for s in range(spans):
            qs = slice(s * SPAN, (s + 1) * SPAN)
            ks = slice(s * keys, (s + 1) * keys)
            scores = dot(q_ref[qs, c], k_ref[ks, c], NT) * scale
            e = jnp.exp(scores - jnp.max(scores, axis=-1, keepdims=True))
            probs = e / jnp.sum(e, axis=-1, keepdims=True)
            p_ref[j, s] = probs
            a_ref[qs, c] = dot(probs.astype(BF16), v_ref[ks, c]).astype(BF16)


def forward_of(t, query, pieces, key_weight, value_weight):
    rows, cols = query.shape
    blocks, part, length = pieces[0].shape
    tokens, width = blocks * length, key_weight.shape[0]
    spans = rows // SPAN
    step = 2 * HEAD
    col = lambda n: pl.BlockSpec((n, step), lambda j, t: (0, j))
    return pl.pallas_call(
        functools.partial(forward_kernel, 1.0 / math.sqrt(HEAD)),
        out_shape=(
            jax.ShapeDtypeStruct((tokens, cols), BF16),
            jax.ShapeDtypeStruct((tokens, cols), BF16),
            jax.ShapeDtypeStruct((cols // HEAD, spans, SPAN, tokens // spans), F32),
            jax.ShapeDtypeStruct((rows, cols), BF16),
        ),
        grid_spec=pltpu.PrefetchScalarGridSpec(
            num_scalar_prefetch=1,
            grid=(cols // step,),
            in_specs=[col(rows)] + [whole(pieces[0].shape)] * 4 + [col(width)] * 2,
            out_specs=[
                col(tokens),
                col(tokens),
                pl.BlockSpec((2, spans, SPAN, tokens // spans), lambda j, t: (j, 0, 0, 0)),
                col(rows),
            ],
            scratch_shapes=[pltpu.VMEM((width, tokens), BF16), pltpu.VMEM((tokens, width), BF16)],
        ),
        compiler_params=params(56),
        cost_estimate=cost(4 * tokens * width * cols, 10e6),
        name="forward",
    )(t, query, *pieces, key_weight, value_weight)


def output_kernel(t_ref, a_ref, g_ref, own, other, o_ref, ga_ref, w_ref, sems):
    core, x = t_ref[1], t_ref[2]
    steps, _, width = g_ref.shape
    chips = own.shape[1]
    deep = own.shape[0] // steps
    copies = []
    for i in range(steps):
        for s in range(chips):
            at = (x - s + chips) % chips
            for n, (plane, c) in enumerate(((own, core), (other, 1 - core))):
                copies.append(
                    pltpu.make_async_copy(
                        plane.at[pl.ds(i * deep, deep), s], w_ref.at[i, :, at, c], sems.at[i, 2 * s + n]
                    )
                )
    for copy in copies:
        copy.start()
    total = None
    for i in range(steps):
        for copy in copies[i * 2 * chips : (i + 1) * 2 * chips]:
            copy.wait()
        w = w_ref[i].reshape(width, a_ref.shape[1])
        part = dot(g_ref[i], w)
        total = part if total is None else total + part
        o_ref[i] = dot(a_ref[...], w, NT).astype(BF16)
    ga_ref[...] = total.astype(BF16)


def output_of(t, attended, pieces, own, other):
    rows, cols = attended.shape
    steps, _, width = pieces.shape
    deep, chips = own.shape[0] // steps, own.shape[1]
    return pl.pallas_call(
        output_kernel,
        out_shape=(
            jax.ShapeDtypeStruct((steps, rows, width), BF16),
            jax.ShapeDtypeStruct((rows, cols), BF16),
        ),
        grid=(1,),
        in_specs=[
            SMEM,
            whole((rows, cols)),
            pl.BlockSpec((steps, rows, width), lambda i: (0, 1, 0)),
            ANY,
            ANY,
        ],
        out_specs=(whole((steps, rows, width)), whole((rows, cols))),
        scratch_shapes=[
            pltpu.VMEM((steps, deep, chips, 2, *own.shape[2:]), BF16),
            pltpu.SemaphoreType.DMA((steps, 2 * chips)),
        ],
        compiler_params=params(28),
        cost_estimate=cost(4 * rows * steps * width * cols, 2 * steps * width * cols),
        name="output",
    )(t, attended, pieces, own, other)


def backward_kernel(
    scale, t_ref, ga_ref, q_ref, k_ref, v_ref, p_ref, kw_ref, vw_ref, gq_ref, s0, s1, s2, s3, gk, gv, acc
):
    j, last = pl.program_id(0), pl.num_programs(0) - 1
    spans = q_ref.shape[0] // SPAN
    keys = k_ref.shape[0] // spans
    for h in range(q_ref.shape[1] // HEAD):
        c = slice(h * HEAD, (h + 1) * HEAD)
        for s in range(spans):
            qs = slice(s * SPAN, (s + 1) * SPAN)
            ks = slice(s * keys, (s + 1) * keys)
            probs, ga = p_ref[h, s], ga_ref[qs, c]
            gp = dot(ga, v_ref[ks, c], NT)
            inner = jnp.sum(probs * gp, axis=-1, keepdims=True)
            gs = (probs * (gp - inner) * scale).astype(BF16)
            gq_ref[qs, c] = dot(gs, k_ref[ks, c]).astype(BF16)
            gk[ks, c] = dot(gs, q_ref[qs, c], TN).astype(BF16)
            gv[ks, c] = dot(probs.astype(BF16), ga, TN).astype(BF16)
    part = dot(kw_ref[...], gk[...], NT) + dot(vw_ref[...], gv[...], NT)

    @pl.when(j == 0)
    def _():
        acc[...] = part

    @pl.when(j > 0)
    def _():
        acc[...] += part

    @pl.when(j == last)
    def _():
        blocks, rows, length = s0.shape
        for r, out in enumerate((s0, s1, s2, s3)):
            at = pl.multiple_of(((t_ref[0] + r) % 4) * rows, rows)
            for b in range(blocks):
                out[b] = acc[pl.ds(at, rows), b * length : (b + 1) * length].astype(BF16)


def backward_of(t, ga, query, key, value, probs, key_weight, value_weight, piece):
    rows, cols = query.shape
    tokens, width = key.shape[0], key_weight.shape[0]
    spans = rows // SPAN
    step = 2 * HEAD
    col = lambda n: pl.BlockSpec((n, step), lambda j, t: (0, j))
    return pl.pallas_call(
        functools.partial(backward_kernel, 1.0 / math.sqrt(HEAD)),
        out_shape=[jax.ShapeDtypeStruct((rows, cols), BF16)] + [jax.ShapeDtypeStruct(piece, BF16)] * 4,
        grid_spec=pltpu.PrefetchScalarGridSpec(
            num_scalar_prefetch=1,
            grid=(cols // step,),
            in_specs=[
                col(rows),
                col(rows),
                col(tokens),
                col(tokens),
                pl.BlockSpec((2, spans, SPAN, tokens // spans), lambda j, t: (j, 0, 0, 0)),
                col(width),
                col(width),
            ],
            out_specs=[col(rows)] + [whole(piece)] * 4,
            scratch_shapes=[
                pltpu.VMEM((tokens, step), BF16),
                pltpu.VMEM((tokens, step), BF16),
                pltpu.VMEM((width, tokens), F32),
            ],
        ),
        compiler_params=params(56),
        cost_estimate=cost(4 * tokens * width * cols, 10e6),
        name="backward",
    )(t, ga, query, key, value, probs, key_weight, value_weight)


def hidden_kernel(g_ref, w_ref, o_ref):
    o_ref[0] = dot(g_ref[...], w_ref[...], NT).astype(BF16)


def hidden_of(grad_query, weight):
    rows, cols = grad_query.shape
    width = weight.shape[0] // 4
    return pl.pallas_call(
        hidden_kernel,
        out_shape=jax.ShapeDtypeStruct((4, rows, width), BF16),
        grid=(4,),
        in_specs=[whole((rows, cols)), pl.BlockSpec((width, cols), lambda i: (i, 0))],
        out_specs=pl.BlockSpec((1, rows, width), lambda i: (i, 0, 0)),
        compiler_params=params(56),
        cost_estimate=cost(2 * rows * 4 * width * cols, 8 * width * cols),
        name="hidden",
    )(grad_query, weight)


def pairs_moved(blocks, gaps, sign):
    n = math.prod(lax.axis_size(a) for a in DP)
    low = jnp.minimum(gaps[0], gaps[1])
    high = jnp.maximum(gaps[0], gaps[1])
    first_low = gaps[0] == low
    pairs = blocks[:2], blocks[2:]

    def moved(x, by):
        return lax.ppermute(x, DP, [(i, (i + sign * by) % n) for i in range(n)])

    choices = list(itertools.combinations(range(1, WINDOW + 1), 2))
    which = sum(i * ((low == a) & (high == b)).astype(jnp.int32) for i, (a, b) in enumerate(choices))
    branches = [lambda x, y, a=a, b=b: (moved(x, a), moved(y, b)) for a, b in choices]
    near, far = lax.switch(
        which, branches, jnp.where(first_low, *pairs), jnp.where(first_low, *pairs[::-1])
    )
    return jnp.concatenate([jnp.where(first_low, near, far), jnp.where(first_low, far, near)], axis=0)


def gathered_plane(rows):
    n = lax.axis_size("x")
    along = [rows]
    for s in range(1, n):
        along.append(lax.ppermute(rows, "x", [(i, (i + s) % n) for i in range(n)]))
    return lax.all_gather(jnp.stack(along), "z", axis=0)


def shards(
    hidden,
    grad_out,
    query_weight,
    key_weight,
    value_weight,
    out_weight,
    neighbour_states,
    block_owner,
    slot_target,
):
    n_dp = math.prod(lax.axis_size(a) for a in DP)
    t = jnp.stack([lax.axis_index(a) for a in ("tensor", "core", "x")]).astype(jnp.int32)
    plane = gathered_plane(out_weight.T)

    gap = (block_owner[0] - lax.axis_index(DP) + n_dp) % n_dp
    gaps = (gap[0], gap[2])
    both = jnp.concatenate([hidden, grad_out], axis=0)
    pieces = exchanged(jnp.broadcast_to(both, (lax.axis_size("tensor"), *both.shape)))
    pieces = pieces.reshape(-1, *both.shape)
    mine = pairs_moved(jnp.swapaxes(neighbour_states, 1, 2), gaps, -1)
    neighbours = from_peers(mine)

    query = query_of(pieces, query_weight)
    key, value, probs, attended = forward_of(t, query, neighbours, key_weight, value_weight)
    plane = tied(plane, attended)
    other_plane = lax.ppermute(plane, "core", [(0, 1), (1, 0)])
    out_parts, grad_attended = output_of(t, attended, pieces, plane, other_plane)
    cross_out = summed(exchanged(out_parts))
    grad_query, *state_parts = backward_of(
        t, grad_attended, query, key, value, probs, key_weight, value_weight, mine.shape
    )
    grad_hidden = summed(exchanged(hidden_of(grad_query, query_weight)))
    grads = summed(to_peers(state_parts))
    grad_states = jnp.swapaxes(pairs_moved(grads, gaps, 1), 1, 2)
    return cross_out, grad_hidden, grad_states


def solution(mesh):
    grid = Mesh(mesh.devices.reshape(8, 4, 2, 4), DP + ("tensor",))
    placed = (
        P(DP, "tensor"),
        P(DP, "tensor"),
        P(None, "tensor"),
        P(None, "tensor"),
        P(None, "tensor"),
        P("tensor", DP),
        P(DP, None, "tensor"),
        P(DP, None),
        P(DP, None),
    )
    return jax.shard_map(
        shards,
        mesh=grid,
        in_specs=placed,
        out_specs=(P(DP, "tensor"), P(DP, "tensor"), P(DP, None, "tensor")),
        check_vma=False,
    )
```

```python
import functools
import itertools
import math

import jax
import jax.numpy as jnp
from jax import lax
from jax.experimental import pallas as pl
from jax.experimental.pallas import tpu as pltpu
from jax.sharding import Mesh, PartitionSpec as P

HEAD = 128
SPAN = 64
NBR = 128
WINDOW = 4
DP = ("z", "x", "core")
MIB = 1024 * 1024
F32, BF16 = jnp.float32, jnp.bfloat16

NN = (((1,), (0,)), ((), ()))
NT = (((1,), (1,)), ((), ()))
TN = (((0,), (0,)), ((), ()))


def dot(a, b, dims=NN):
    return lax.dot_general(a, b, dims, preferred_element_type=F32)


def params(mib):
    return pltpu.CompilerParams(vmem_limit_bytes=mib * MIB)


ANY = pl.BlockSpec(memory_space=pl.ANY)
SMEM = pl.BlockSpec(memory_space=pltpu.SMEM)


def whole(shape):
    return pl.BlockSpec(shape, lambda *_: (0,) * len(shape))


def cost(flops, nbytes):
    return pl.CostEstimate(flops=int(flops), bytes_accessed=int(nbytes), transcendentals=0)


def from_peers(x):
    n = lax.axis_size("tensor")
    got = [x]
    for r in range(1, n):
        got.append(lax.ppermute(x, "tensor", [((i + r) % n, i) for i in range(n)]))
    return got


def to_peers(pieces):
    n = lax.axis_size("tensor")
    got = [pieces[0]]
    for r in range(1, n):
        got.append(lax.ppermute(pieces[r], "tensor", [(i, (i + r) % n) for i in range(n)]))
    return got


def exchanged(x):
    return lax.all_to_all(x, "tensor", split_axis=0, concat_axis=0, tiled=True)


def summed(parts):
    total = parts[0].astype(F32)
    for part in parts[1:]:
        total = total + part.astype(F32)
    return total.astype(BF16)


def nothing(*_):
    pass


def tied(x, *after):
    return pl.pallas_call(
        nothing,
        out_shape=jax.ShapeDtypeStruct(x.shape, x.dtype),
        in_specs=[ANY] * (1 + len(after)),
        out_specs=ANY,
        input_output_aliases={0: 0},
        name="tied",
    )(x, *after)


def query_kernel(h_ref, w_ref, q_ref, acc):
    i, last = pl.program_id(0), pl.num_programs(0) - 1
    part = dot(h_ref[0], w_ref[...])

    @pl.when(i == 0)
    def _():
        acc[...] = part

    @pl.when(jnp.logical_and(i > 0, i < last))
    def _():
        acc[...] += part

    @pl.when(i == last)
    def _():
        q_ref[...] = (acc[...] + part).astype(BF16)


def query_of(pieces, weight):
    steps, rows, width = pieces.shape
    rows, cols = rows // 2, weight.shape[1]
    return pl.pallas_call(
        query_kernel,
        out_shape=jax.ShapeDtypeStruct((rows, cols), BF16),
        grid=(steps,),
        in_specs=[
            pl.BlockSpec((1, rows, width), lambda i: (i, 0, 0)),
            pl.BlockSpec((width, cols), lambda i: (i, 0)),
        ],
        out_specs=whole((rows, cols)),
        scratch_shapes=[pltpu.VMEM((rows, cols), F32)],
        compiler_params=params(56),
        cost_estimate=cost(2 * rows * steps * width * cols, 2 * steps * width * cols),
        name="query",
    )(pieces, weight)


def forward_kernel(
    scale, t_ref, q_ref, n0, n1, n2, n3, kw_ref, vw_ref, k_ref, v_ref, p_ref, a_ref, flipped, rows
):
    blocks, part, length = n0.shape

    @pl.when(pl.program_id(0) == 0)
    def _():
        for r, n in enumerate((n0, n1, n2, n3)):
            at = pl.multiple_of(((t_ref[0] + r) % 4) * part, part)
            for b in range(blocks):
                flipped[pl.ds(at, part), b * length : (b + 1) * length] = n[b]
        rows[...] = flipped[...].T

    k_ref[...] = dot(rows[...], kw_ref[...]).astype(BF16)
    v_ref[...] = dot(rows[...], vw_ref[...]).astype(BF16)
    spans = q_ref.shape[0] // SPAN
    keys = k_ref.shape[0] // spans
    for j in range(q_ref.shape[1] // HEAD):
        c = slice(j * HEAD, (j + 1) * HEAD)
        for s in range(spans):
            qs = slice(s * SPAN, (s + 1) * SPAN)
            ks = slice(s * keys, (s + 1) * keys)
            scores = dot(q_ref[qs, c], k_ref[ks, c], NT) * scale
            e = jnp.exp(scores - jnp.max(scores, axis=-1, keepdims=True))
            probs = e / jnp.sum(e, axis=-1, keepdims=True)
            p_ref[j, s] = probs
            a_ref[qs, c] = dot(probs.astype(BF16), v_ref[ks, c]).astype(BF16)


def forward_of(t, query, pieces, key_weight, value_weight):
    rows, cols = query.shape
    blocks, part, length = pieces[0].shape
    tokens, width = blocks * length, key_weight.shape[0]
    spans = rows // SPAN
    step = 2 * HEAD
    col = lambda n: pl.BlockSpec((n, step), lambda j, t: (0, j))
    return pl.pallas_call(
        functools.partial(forward_kernel, 1.0 / math.sqrt(HEAD)),
        out_shape=(
            jax.ShapeDtypeStruct((tokens, cols), BF16),
            jax.ShapeDtypeStruct((tokens, cols), BF16),
            jax.ShapeDtypeStruct((cols // HEAD, spans, SPAN, tokens // spans), F32),
            jax.ShapeDtypeStruct((rows, cols), BF16),
        ),
        grid_spec=pltpu.PrefetchScalarGridSpec(
            num_scalar_prefetch=1,
            grid=(cols // step,),
            in_specs=[col(rows)] + [whole(pieces[0].shape)] * 4 + [col(width)] * 2,
            out_specs=[
                col(tokens),
                col(tokens),
                pl.BlockSpec((2, spans, SPAN, tokens // spans), lambda j, t: (j, 0, 0, 0)),
                col(rows),
            ],
            scratch_shapes=[pltpu.VMEM((width, tokens), BF16), pltpu.VMEM((tokens, width), BF16)],
        ),
        compiler_params=params(56),
        cost_estimate=cost(4 * tokens * width * cols, 10e6),
        name="forward",
    )(t, query, *pieces, key_weight, value_weight)


def output_kernel(first, t_ref, a_ref, g_ref, w_ref, *refs):
    if not first:
        o_before, ga_before, *refs = refs
    o_ref, ga_ref, pick, acc = refs
    i, last = pl.program_id(0), pl.num_programs(0) - 1
    deep, chips, group, cols = w_ref.shape
    rows, width = g_ref.shape[1], chips * group

    @pl.when(i == 0)
    def _():
        core = t_ref[1] if first else 1 - t_ref[1]
        full = lax.broadcasted_iota(jnp.int32, pick.shape, 0)
        part = lax.broadcasted_iota(jnp.int32, pick.shape, 1)
        chip = (t_ref[2] - part // group + chips) % chips
        pick[...] = jnp.where(full == chip * 2 * group + core * group + part % group, 1.0, 0.0).astype(BF16)
        acc[...] = jnp.zeros_like(acc) if first else ga_before[...]

    both = jnp.concatenate([g_ref[0, :, : 2 * width], g_ref[0, :, 2 * width :]], axis=0)
    picked = dot(both, pick[...]).astype(BF16)
    total, outs = acc[...], []
    for z in range(deep):
        w = w_ref[z].reshape(width, cols)
        total = total + dot(picked[z * rows : (z + 1) * rows], w)
        outs.append(dot(a_ref[...], w, NT).astype(BF16))
    acc[...] = total
    placed = dot(jnp.concatenate(outs, axis=0), pick[...], NT)
    for z in range(deep):
        at = slice(z * 2 * width, (z + 1) * 2 * width)
        out = placed[z * rows : (z + 1) * rows]
        o_ref[0, :, at] = (out if first else out + o_before[0, :, at].astype(F32)).astype(BF16)

    @pl.when(i == last)
    def _():
        ga_ref[...] = total.astype(ga_ref.dtype)


def output_of(t, attended, pieces, plane, before=()):
    rows, cols = attended.shape
    steps, _, width = pieces.shape
    first = not before
    block = pl.BlockSpec((1, rows, width), lambda i: (i, 0, 0))
    deep = plane.shape[0] // steps
    return pl.pallas_call(
        functools.partial(output_kernel, first),
        out_shape=(
            jax.ShapeDtypeStruct((steps, rows, width), BF16),
            jax.ShapeDtypeStruct((rows, cols), F32 if first else BF16),
        ),
        grid=(steps,),
        in_specs=[
            SMEM,
            whole((rows, cols)),
            pl.BlockSpec((1, rows, width), lambda i: (i, 1, 0)),
            pl.BlockSpec((deep, *plane.shape[1:]), lambda i: (i, 0, 0, 0)),
        ]
        + ([] if first else [block, whole((rows, cols))]),
        out_specs=(block, whole((rows, cols))),
        scratch_shapes=[
            pltpu.VMEM((width // deep, width // deep // 2), BF16),
            pltpu.VMEM((rows, cols), F32),
        ],
        compiler_params=params(28),
        cost_estimate=cost(2 * rows * steps * width * cols, steps * width * cols),
        name="output",
    )(t, attended, pieces, plane, *before)


def backward_kernel(
    scale, t_ref, ga_ref, q_ref, k_ref, v_ref, p_ref, kw_ref, vw_ref, gq_ref, s0, s1, s2, s3, gk, gv, acc
):
    j, last = pl.program_id(0), pl.num_programs(0) - 1
    spans = q_ref.shape[0] // SPAN
    keys = k_ref.shape[0] // spans
    for h in range(q_ref.shape[1] // HEAD):
        c = slice(h * HEAD, (h + 1) * HEAD)
        for s in range(spans):
            qs = slice(s * SPAN, (s + 1) * SPAN)
            ks = slice(s * keys, (s + 1) * keys)
            probs, ga = p_ref[h, s], ga_ref[qs, c]
            gp = dot(ga, v_ref[ks, c], NT)
            inner = jnp.sum(probs * gp, axis=-1, keepdims=True)
            gs = (probs * (gp - inner) * scale).astype(BF16)
            gq_ref[qs, c] = dot(gs, k_ref[ks, c]).astype(BF16)
            gk[ks, c] = dot(gs, q_ref[qs, c], TN).astype(BF16)
            gv[ks, c] = dot(probs.astype(BF16), ga, TN).astype(BF16)
    part = dot(kw_ref[...], gk[...], NT) + dot(vw_ref[...], gv[...], NT)

    @pl.when(j == 0)
    def _():
        acc[...] = part

    @pl.when(j > 0)
    def _():
        acc[...] += part

    @pl.when(j == last)
    def _():
        blocks, rows, length = s0.shape
        for r, out in enumerate((s0, s1, s2, s3)):
            at = pl.multiple_of(((t_ref[0] + r) % 4) * rows, rows)
            for b in range(blocks):
                out[b] = acc[pl.ds(at, rows), b * length : (b + 1) * length].astype(BF16)


def backward_of(t, ga, query, key, value, probs, key_weight, value_weight, piece):
    rows, cols = query.shape
    tokens, width = key.shape[0], key_weight.shape[0]
    spans = rows // SPAN
    step = 2 * HEAD
    col = lambda n: pl.BlockSpec((n, step), lambda j, t: (0, j))
    return pl.pallas_call(
        functools.partial(backward_kernel, 1.0 / math.sqrt(HEAD)),
        out_shape=[jax.ShapeDtypeStruct((rows, cols), BF16)] + [jax.ShapeDtypeStruct(piece, BF16)] * 4,
        grid_spec=pltpu.PrefetchScalarGridSpec(
            num_scalar_prefetch=1,
            grid=(cols // step,),
            in_specs=[
                col(rows),
                col(rows),
                col(tokens),
                col(tokens),
                pl.BlockSpec((2, spans, SPAN, tokens // spans), lambda j, t: (j, 0, 0, 0)),
                col(width),
                col(width),
            ],
            out_specs=[col(rows)] + [whole(piece)] * 4,
            scratch_shapes=[
                pltpu.VMEM((tokens, step), BF16),
                pltpu.VMEM((tokens, step), BF16),
                pltpu.VMEM((width, tokens), F32),
            ],
        ),
        compiler_params=params(56),
        cost_estimate=cost(4 * tokens * width * cols, 10e6),
        name="backward",
    )(t, ga, query, key, value, probs, key_weight, value_weight)


def hidden_kernel(g_ref, w_ref, o_ref):
    o_ref[0] = dot(g_ref[...], w_ref[...], NT).astype(BF16)


def hidden_of(grad_query, weight):
    rows, cols = grad_query.shape
    width = weight.shape[0] // 4
    return pl.pallas_call(
        hidden_kernel,
        out_shape=jax.ShapeDtypeStruct((4, rows, width), BF16),
        grid=(4,),
        in_specs=[whole((rows, cols)), pl.BlockSpec((width, cols), lambda i: (i, 0))],
        out_specs=pl.BlockSpec((1, rows, width), lambda i: (i, 0, 0)),
        compiler_params=params(56),
        cost_estimate=cost(2 * rows * 4 * width * cols, 8 * width * cols),
        name="hidden",
    )(grad_query, weight)


def pairs_moved(blocks, gaps, sign):
    n = math.prod(lax.axis_size(a) for a in DP)
    low = jnp.minimum(gaps[0], gaps[1])
    high = jnp.maximum(gaps[0], gaps[1])
    first_low = gaps[0] == low
    pairs = blocks[:2], blocks[2:]

    def moved(x, by):
        return lax.ppermute(x, DP, [(i, (i + sign * by) % n) for i in range(n)])

    choices = list(itertools.combinations(range(1, WINDOW + 1), 2))
    which = sum(i * ((low == a) & (high == b)).astype(jnp.int32) for i, (a, b) in enumerate(choices))
    branches = [lambda x, y, a=a, b=b: (moved(x, a), moved(y, b)) for a, b in choices]
    near, far = lax.switch(
        which, branches, jnp.where(first_low, *pairs), jnp.where(first_low, *pairs[::-1])
    )
    return jnp.concatenate([jnp.where(first_low, near, far), jnp.where(first_low, far, near)], axis=0)


def gathered_plane(rows):
    n = lax.axis_size("x")
    along = [rows]
    for s in range(1, n):
        along.append(lax.ppermute(rows, "x", [(i, (i + s) % n) for i in range(n)]))
    return lax.all_gather(jnp.stack(along), "z", axis=0)


def shards(
    hidden,
    grad_out,
    query_weight,
    key_weight,
    value_weight,
    out_weight,
    neighbour_states,
    block_owner,
    slot_target,
):
    n_dp = math.prod(lax.axis_size(a) for a in DP)
    t = jnp.stack([lax.axis_index(a) for a in ("tensor", "core", "x")]).astype(jnp.int32)
    plane = gathered_plane(out_weight.T)

    gap = (block_owner[0] - lax.axis_index(DP) + n_dp) % n_dp
    gaps = (gap[0], gap[2])
    both = jnp.concatenate([hidden, grad_out], axis=0)
    pieces = exchanged(jnp.broadcast_to(both, (lax.axis_size("tensor"), *both.shape)))
    pieces = pieces.reshape(-1, *both.shape)
    mine = pairs_moved(jnp.swapaxes(neighbour_states, 1, 2), gaps, -1)
    neighbours = from_peers(mine)

    query = query_of(pieces, query_weight)
    key, value, probs, attended = forward_of(t, query, neighbours, key_weight, value_weight)
    plane = tied(plane, attended)
    other_plane = lax.ppermute(plane, "core", [(0, 1), (1, 0)])
    before = output_of(t, attended, pieces, plane)
    out_parts, grad_attended = output_of(t, attended, pieces, other_plane, before)
    cross_out = summed(exchanged(out_parts))
    grad_query, *state_parts = backward_of(
        t, grad_attended, query, key, value, probs, key_weight, value_weight, mine.shape
    )
    grad_hidden = summed(exchanged(hidden_of(grad_query, query_weight)))
    grads = summed(to_peers(state_parts))
    grad_states = jnp.swapaxes(pairs_moved(grads, gaps, 1), 1, 2)
    return cross_out, grad_hidden, grad_states


def solution(mesh):
    grid = Mesh(mesh.devices.reshape(8, 4, 2, 4), DP + ("tensor",))
    placed = (
        P(DP, "tensor"),
        P(DP, "tensor"),
        P(None, "tensor"),
        P(None, "tensor"),
        P(None, "tensor"),
        P("tensor", DP),
        P(DP, None, "tensor"),
        P(DP, None),
        P(DP, None),
    )
    return jax.shard_map(
        shards,
        mesh=grid,
        in_specs=placed,
        out_specs=(P(DP, "tensor"), P(DP, "tensor"), P(DP, None, "tensor")),
        check_vma=False,
    )
```

```python
import functools
import itertools
import math

import jax
import jax.numpy as jnp
from jax import lax
from jax.experimental import pallas as pl
from jax.experimental.pallas import tpu as pltpu
from jax.sharding import Mesh, PartitionSpec as P

HEAD = 128
SPAN = 64
NBR = 128
WINDOW = 4
DP = ("z", "x", "core")
MIB = 1024 * 1024
F32, BF16 = jnp.float32, jnp.bfloat16

NN = (((1,), (0,)), ((), ()))
NT = (((1,), (1,)), ((), ()))
TN = (((0,), (0,)), ((), ()))


def dot(a, b, dims=NN):
    return lax.dot_general(a, b, dims, preferred_element_type=F32)


def params(mib):
    return pltpu.CompilerParams(vmem_limit_bytes=mib * MIB)


ANY = pl.BlockSpec(memory_space=pl.ANY)
SMEM = pl.BlockSpec(memory_space=pltpu.SMEM)


def whole(shape):
    return pl.BlockSpec(shape, lambda *_: (0,) * len(shape))


def cost(flops, nbytes):
    return pl.CostEstimate(flops=int(flops), bytes_accessed=int(nbytes), transcendentals=0)


def from_peers(x):
    n = lax.axis_size("tensor")
    got = [x]
    for r in range(1, n):
        got.append(lax.ppermute(x, "tensor", [((i + r) % n, i) for i in range(n)]))
    return got


def to_peers(pieces):
    n = lax.axis_size("tensor")
    got = [pieces[0]]
    for r in range(1, n):
        got.append(lax.ppermute(pieces[r], "tensor", [(i, (i + r) % n) for i in range(n)]))
    return got


def exchanged(x):
    return lax.all_to_all(x, "tensor", split_axis=0, concat_axis=0, tiled=True)


def summed(parts):
    total = parts[0].astype(F32)
    for part in parts[1:]:
        total = total + part.astype(F32)
    return total.astype(BF16)


def nothing(*_):
    pass


def tied(x, *after):
    return pl.pallas_call(
        nothing,
        out_shape=jax.ShapeDtypeStruct(x.shape, x.dtype),
        in_specs=[ANY] * (1 + len(after)),
        out_specs=ANY,
        input_output_aliases={0: 0},
        name="tied",
    )(x, *after)


def query_kernel(h_ref, w_ref, q_ref, acc):
    i, last = pl.program_id(0), pl.num_programs(0) - 1
    part = dot(h_ref[0], w_ref[...])

    @pl.when(i == 0)
    def _():
        acc[...] = part

    @pl.when(jnp.logical_and(i > 0, i < last))
    def _():
        acc[...] += part

    @pl.when(i == last)
    def _():
        q_ref[...] = (acc[...] + part).astype(BF16)


def query_of(pieces, weight):
    steps, rows, width = pieces.shape
    rows, cols = rows // 2, weight.shape[1]
    return pl.pallas_call(
        query_kernel,
        out_shape=jax.ShapeDtypeStruct((rows, cols), BF16),
        grid=(steps,),
        in_specs=[
            pl.BlockSpec((1, rows, width), lambda i: (i, 0, 0)),
            pl.BlockSpec((width, cols), lambda i: (i, 0)),
        ],
        out_specs=whole((rows, cols)),
        scratch_shapes=[pltpu.VMEM((rows, cols), F32)],
        compiler_params=params(56),
        cost_estimate=cost(2 * rows * steps * width * cols, 2 * steps * width * cols),
        name="query",
    )(pieces, weight)


def forward_kernel(
    scale, t_ref, q_ref, n0, n1, n2, n3, kw_ref, vw_ref, k_ref, v_ref, p_ref, a_ref, flipped, rows
):
    blocks, part, length = n0.shape

    @pl.when(pl.program_id(0) == 0)
    def _():
        for r, n in enumerate((n0, n1, n2, n3)):
            at = pl.multiple_of(((t_ref[0] + r) % 4) * part, part)
            for b in range(blocks):
                flipped[pl.ds(at, part), b * length : (b + 1) * length] = n[b]
        rows[...] = flipped[...].T

    k_ref[...] = dot(rows[...], kw_ref[...]).astype(BF16)
    v_ref[...] = dot(rows[...], vw_ref[...]).astype(BF16)
    spans = q_ref.shape[0] // SPAN
    keys = k_ref.shape[0] // spans
    for j in range(q_ref.shape[1] // HEAD):
        c = slice(j * HEAD, (j + 1) * HEAD)
        for s in range(spans):
            qs = slice(s * SPAN, (s + 1) * SPAN)
            ks = slice(s * keys, (s + 1) * keys)
            scores = dot(q_ref[qs, c], k_ref[ks, c], NT) * scale
            e = jnp.exp(scores - jnp.max(scores, axis=-1, keepdims=True))
            probs = e / jnp.sum(e, axis=-1, keepdims=True)
            p_ref[j, s] = probs
            a_ref[qs, c] = dot(probs.astype(BF16), v_ref[ks, c]).astype(BF16)


def forward_of(t, query, pieces, key_weight, value_weight):
    rows, cols = query.shape
    blocks, part, length = pieces[0].shape
    tokens, width = blocks * length, key_weight.shape[0]
    spans = rows // SPAN
    step = 2 * HEAD
    col = lambda n: pl.BlockSpec((n, step), lambda j, t: (0, j))
    return pl.pallas_call(
        functools.partial(forward_kernel, 1.0 / math.sqrt(HEAD)),
        out_shape=(
            jax.ShapeDtypeStruct((tokens, cols), BF16),
            jax.ShapeDtypeStruct((tokens, cols), BF16),
            jax.ShapeDtypeStruct((cols // HEAD, spans, SPAN, tokens // spans), F32),
            jax.ShapeDtypeStruct((rows, cols), BF16),
        ),
        grid_spec=pltpu.PrefetchScalarGridSpec(
            num_scalar_prefetch=1,
            grid=(cols // step,),
            in_specs=[col(rows)] + [whole(pieces[0].shape)] * 4 + [col(width)] * 2,
            out_specs=[
                col(tokens),
                col(tokens),
                pl.BlockSpec((2, spans, SPAN, tokens // spans), lambda j, t: (j, 0, 0, 0)),
                col(rows),
            ],
            scratch_shapes=[pltpu.VMEM((width, tokens), BF16), pltpu.VMEM((tokens, width), BF16)],
        ),
        compiler_params=params(56),
        cost_estimate=cost(4 * tokens * width * cols, 10e6),
        name="forward",
    )(t, query, *pieces, key_weight, value_weight)


def output_kernel(first, t_ref, a_ref, g_ref, w_ref, *refs):
    if not first:
        o_before, ga_before, *refs = refs
    o_ref, ga_ref, pick, acc = refs
    i, last = pl.program_id(0), pl.num_programs(0) - 1
    deep, chips, group, cols = w_ref.shape
    rows, width = g_ref.shape[1], chips * group

    @pl.when(i == 0)
    def _():
        core = t_ref[1] if first else 1 - t_ref[1]
        full = lax.broadcasted_iota(jnp.int32, pick.shape, 0)
        part = lax.broadcasted_iota(jnp.int32, pick.shape, 1)
        chip = (t_ref[2] - part // group + chips) % chips
        pick[...] = jnp.where(full == chip * 2 * group + core * group + part % group, 1.0, 0.0).astype(BF16)
        acc[...] = jnp.zeros_like(acc) if first else ga_before[...]

    both = jnp.concatenate([g_ref[0, :, : 2 * width], g_ref[0, :, 2 * width :]], axis=0)
    picked = dot(both, pick[...]).astype(BF16)
    total, outs = acc[...], []
    for z in range(deep):
        w = w_ref[z].reshape(width, cols)
        total = total + dot(picked[z * rows : (z + 1) * rows], w)
        outs.append(dot(a_ref[...], w, NT).astype(BF16))
    acc[...] = total
    placed = dot(jnp.concatenate(outs, axis=0), pick[...], NT)
    for z in range(deep):
        at = slice(z * 2 * width, (z + 1) * 2 * width)
        out = placed[z * rows : (z + 1) * rows]
        o_ref[0, :, at] = (out if first else out + o_before[0, :, at].astype(F32)).astype(BF16)

    @pl.when(i == last)
    def _():
        ga_ref[...] = total.astype(ga_ref.dtype)


def output_of(t, attended, pieces, plane, before=()):
    rows, cols = attended.shape
    steps, _, width = pieces.shape
    first = not before
    block = pl.BlockSpec((1, rows, width), lambda i: (i, 0, 0))
    deep = plane.shape[0] // steps
    return pl.pallas_call(
        functools.partial(output_kernel, first),
        out_shape=(
            jax.ShapeDtypeStruct((steps, rows, width), BF16),
            jax.ShapeDtypeStruct((rows, cols), F32 if first else BF16),
        ),
        grid=(steps,),
        in_specs=[
            SMEM,
            whole((rows, cols)),
            pl.BlockSpec((1, rows, width), lambda i: (i, 1, 0)),
            pl.BlockSpec((deep, *plane.shape[1:]), lambda i: (i, 0, 0, 0)),
        ]
        + ([] if first else [block, whole((rows, cols))]),
        out_specs=(block, whole((rows, cols))),
        scratch_shapes=[
            pltpu.VMEM((width // deep, width // deep // 2), BF16),
            pltpu.VMEM((rows, cols), F32),
        ],
        compiler_params=params(56 if first else 28),
        cost_estimate=cost(2 * rows * steps * width * cols, steps * width * cols),
        name="output",
    )(t, attended, pieces, plane, *before)


def backward_kernel(
    scale, t_ref, ga_ref, q_ref, k_ref, v_ref, p_ref, kw_ref, vw_ref, gq_ref, s0, s1, s2, s3, gk, gv, acc
):
    j, last = pl.program_id(0), pl.num_programs(0) - 1
    spans = q_ref.shape[0] // SPAN
    keys = k_ref.shape[0] // spans
    for h in range(q_ref.shape[1] // HEAD):
        c = slice(h * HEAD, (h + 1) * HEAD)
        for s in range(spans):
            qs = slice(s * SPAN, (s + 1) * SPAN)
            ks = slice(s * keys, (s + 1) * keys)
            probs, ga = p_ref[h, s], ga_ref[qs, c]
            gp = dot(ga, v_ref[ks, c], NT)
            inner = jnp.sum(probs * gp, axis=-1, keepdims=True)
            gs = (probs * (gp - inner) * scale).astype(BF16)
            gq_ref[qs, c] = dot(gs, k_ref[ks, c]).astype(BF16)
            gk[ks, c] = dot(gs, q_ref[qs, c], TN).astype(BF16)
            gv[ks, c] = dot(probs.astype(BF16), ga, TN).astype(BF16)
    part = dot(kw_ref[...], gk[...], NT) + dot(vw_ref[...], gv[...], NT)

    @pl.when(j == 0)
    def _():
        acc[...] = part

    @pl.when(j > 0)
    def _():
        acc[...] += part

    @pl.when(j == last)
    def _():
        blocks, rows, length = s0.shape
        for r, out in enumerate((s0, s1, s2, s3)):
            at = pl.multiple_of(((t_ref[0] + r) % 4) * rows, rows)
            for b in range(blocks):
                out[b] = acc[pl.ds(at, rows), b * length : (b + 1) * length].astype(BF16)


def backward_of(t, ga, query, key, value, probs, key_weight, value_weight, piece):
    rows, cols = query.shape
    tokens, width = key.shape[0], key_weight.shape[0]
    spans = rows // SPAN
    step = 2 * HEAD
    col = lambda n: pl.BlockSpec((n, step), lambda j, t: (0, j))
    return pl.pallas_call(
        functools.partial(backward_kernel, 1.0 / math.sqrt(HEAD)),
        out_shape=[jax.ShapeDtypeStruct((rows, cols), BF16)] + [jax.ShapeDtypeStruct(piece, BF16)] * 4,
        grid_spec=pltpu.PrefetchScalarGridSpec(
            num_scalar_prefetch=1,
            grid=(cols // step,),
            in_specs=[
                col(rows),
                col(rows),
                col(tokens),
                col(tokens),
                pl.BlockSpec((2, spans, SPAN, tokens // spans), lambda j, t: (j, 0, 0, 0)),
                col(width),
                col(width),
            ],
            out_specs=[col(rows)] + [whole(piece)] * 4,
            scratch_shapes=[
                pltpu.VMEM((tokens, step), BF16),
                pltpu.VMEM((tokens, step), BF16),
                pltpu.VMEM((width, tokens), F32),
            ],
        ),
        compiler_params=params(56),
        cost_estimate=cost(4 * tokens * width * cols, 10e6),
        name="backward",
    )(t, ga, query, key, value, probs, key_weight, value_weight)


def hidden_kernel(g_ref, w_ref, o_ref):
    o_ref[0] = dot(g_ref[...], w_ref[...], NT).astype(BF16)


def hidden_of(grad_query, weight):
    rows, cols = grad_query.shape
    width = weight.shape[0] // 4
    return pl.pallas_call(
        hidden_kernel,
        out_shape=jax.ShapeDtypeStruct((4, rows, width), BF16),
        grid=(4,),
        in_specs=[whole((rows, cols)), pl.BlockSpec((width, cols), lambda i: (i, 0))],
        out_specs=pl.BlockSpec((1, rows, width), lambda i: (i, 0, 0)),
        compiler_params=params(56),
        cost_estimate=cost(2 * rows * 4 * width * cols, 8 * width * cols),
        name="hidden",
    )(grad_query, weight)


def pairs_moved(blocks, gaps, sign):
    n = math.prod(lax.axis_size(a) for a in DP)
    low = jnp.minimum(gaps[0], gaps[1])
    high = jnp.maximum(gaps[0], gaps[1])
    first_low = gaps[0] == low
    pairs = blocks[:2], blocks[2:]

    def moved(x, by):
        return lax.ppermute(x, DP, [(i, (i + sign * by) % n) for i in range(n)])

    choices = list(itertools.combinations(range(1, WINDOW + 1), 2))
    which = sum(i * ((low == a) & (high == b)).astype(jnp.int32) for i, (a, b) in enumerate(choices))
    branches = [lambda x, y, a=a, b=b: (moved(x, a), moved(y, b)) for a, b in choices]
    near, far = lax.switch(
        which, branches, jnp.where(first_low, *pairs), jnp.where(first_low, *pairs[::-1])
    )
    return jnp.concatenate([jnp.where(first_low, near, far), jnp.where(first_low, far, near)], axis=0)


def gathered_plane(rows):
    n = lax.axis_size("x")
    along = [rows]
    for s in range(1, n):
        along.append(lax.ppermute(rows, "x", [(i, (i + s) % n) for i in range(n)]))
    return lax.all_gather(jnp.stack(along), "z", axis=0)


def shards(
    hidden,
    grad_out,
    query_weight,
    key_weight,
    value_weight,
    out_weight,
    neighbour_states,
    block_owner,
    slot_target,
):
    n_dp = math.prod(lax.axis_size(a) for a in DP)
    t = jnp.stack([lax.axis_index(a) for a in ("tensor", "core", "x")]).astype(jnp.int32)
    plane = gathered_plane(out_weight.T)

    gap = (block_owner[0] - lax.axis_index(DP) + n_dp) % n_dp
    gaps = (gap[0], gap[2])
    both = jnp.concatenate([hidden, grad_out], axis=0)
    pieces = exchanged(jnp.broadcast_to(both, (lax.axis_size("tensor"), *both.shape)))
    pieces = pieces.reshape(-1, *both.shape)
    mine = pairs_moved(jnp.swapaxes(neighbour_states, 1, 2), gaps, -1)
    neighbours = from_peers(mine)

    query = query_of(pieces, query_weight)
    key, value, probs, attended = forward_of(t, query, neighbours, key_weight, value_weight)
    plane = tied(plane, attended)
    other_plane = lax.ppermute(plane, "core", [(0, 1), (1, 0)])
    before = output_of(t, attended, pieces, plane)
    out_parts, grad_attended = output_of(t, attended, pieces, other_plane, before)
    cross_out = summed(exchanged(out_parts))
    grad_query, *state_parts = backward_of(
        t, grad_attended, query, key, value, probs, key_weight, value_weight, mine.shape
    )
    grad_hidden = summed(exchanged(hidden_of(grad_query, query_weight)))
    grads = summed(to_peers(state_parts))
    grad_states = jnp.swapaxes(pairs_moved(grads, gaps, 1), 1, 2)
    return cross_out, grad_hidden, grad_states


def solution(mesh):
    grid = Mesh(mesh.devices.reshape(8, 4, 2, 4), DP + ("tensor",))
    placed = (
        P(DP, "tensor"),
        P(DP, "tensor"),
        P(None, "tensor"),
        P(None, "tensor"),
        P(None, "tensor"),
        P("tensor", DP),
        P(DP, None, "tensor"),
        P(DP, None),
        P(DP, None),
    )
    return jax.shard_map(
        shards,
        mesh=grid,
        in_specs=placed,
        out_specs=(P(DP, "tensor"), P(DP, "tensor"), P(DP, None, "tensor")),
        check_vma=False,
    )
```
